128 devices in a mesh: facet: 8 (over y, z_hi), sub: 16 (over z_lo, x, core).
Axes of the slice: x: 4, y: 4, z: 4 (z_hi: 2, z_lo: 2; z = z_hi * 2 + z_lo), core: 2. Of those that a mesh axis runs over, the one named last changes fastest.
Arguments:
- facet_slab: bfloat16 [256, 2, 65536], P('sub', None, 'facet'), may hold values from -6 to 6
- window: float32 [8192], replicated, may hold values from 0.1 to 1
- facet_offsets: int32 [8], replicated, may hold values from 0 to 7, each once
- subgrid_offsets: int32 [8], replicated, may hold values from 0 to 65535
- row_positions: int32 [256], replicated, may hold values from 0 to 65535
- band_offset: int32 [1], replicated, may hold values from 0 to 65535
- mask_extents: int32 [8, 2], replicated, may hold values from 0 to 511
Outputs:
- subgrid_rows: float32 [128, 8, 2, 2048], P('sub', 'facet')
The draws below stay inside these ranges and needn't reach their ends.
All inputs are finite; a program needn't handle non-finite values.
Results may differ from the reference program's by a relative error of at most 0.0052.
Values may be sent and summed in bfloat16 or wider, within the bound.
A program may use at most 128 MiB of HBM per device.

```python
import math
import jax
import jax.numpy as jnp
from jax import lax

IMAGE = 65536
FS = 8192
SG = 2048
Q = 8
ROWS_TOTAL = 256
SGROWS = 128
N_FACET = 8


def place_ends(result, rng, smallest, high):
    shape = result.shape
    place = [jax.random.randint(jax.random.fold_in(rng, axis), (), 0, shape[axis]) for axis in range(len(shape))]
    result = result.at[tuple(place)].set(smallest)
    longest = shape.index(max(shape))
    place[longest] = (place[longest] + 1) % shape[longest]
    return result.at[tuple(place)].set(high)


def block_levels(rng, dims, shards, low, top_value):
    def one(dim, shards_of):
        draws = jax.random.uniform(jax.random.fold_in(jax.random.fold_in(rng, 6), dim), (shards_of,), jnp.float32, low / len(shards), top_value / len(shards))
        return jnp.repeat(jnp.exp(draws), dims[dim] // shards_of).reshape((-1,) + (1,) * (len(dims) - dim - 1))

    loudness = one(*shards[0])
    for cut in shards[1:]:
        loudness = loudness * one(*cut)
    return loudness


def noise(key, dims, spread, bound, cuts=(), held_as=jnp.bfloat16):
    drawn = jax.random.normal(key, dims, jnp.float32) * spread
    if len(cuts) > 0:
        drawn = block_levels(key, dims, cuts, -0.22, 0.18) * drawn
    return jnp.clip(drawn, min=-bound, max=bound).astype(held_as)


def setup_inputs(seed: int = 0) -> dict:
    splits = jax.random.split(jax.random.key(seed), 8)
    facet_slab = noise(splits[0], (ROWS_TOTAL, 2, N_FACET * FS), 1.0, 6.0, ((0, 16), (2, 8)))
    window = jnp.clip(jnp.exp(jax.random.uniform(splits[1], (FS,), jnp.float32, math.log(0.1), math.log(1.0))), 0.1, 1.0)
    facet_offsets = jax.random.permutation(splits[2], N_FACET).astype(jnp.int32)
    subgrid_offsets = place_ends(jax.random.randint(splits[3], (Q,), 0, IMAGE), jax.random.fold_in(splits[3], 1), 0, IMAGE - 1).astype(jnp.int32)
    row_positions = place_ends(jax.random.randint(splits[4], (ROWS_TOTAL,), 0, IMAGE), jax.random.fold_in(splits[4], 1), 0, IMAGE - 1).astype(jnp.int32)
    band_offset = jax.random.randint(splits[5], (1,), 0, IMAGE).astype(jnp.int32)
    mask_extents = place_ends(jax.random.randint(splits[6], (Q, 2), 0, SG // 4), jax.random.fold_in(splits[6], 1), 0, (SG // 4) - 1).astype(jnp.int32)
    return dict(facet_slab=facet_slab, window=window, facet_offsets=facet_offsets, subgrid_offsets=subgrid_offsets, row_positions=row_positions, band_offset=band_offset, mask_extents=mask_extents)


TWO_PI = 2.0 * math.pi

def mul_mod(left, right, modulus):
    right = right % modulus
    high_part = left // 256
    low_part = left % 256
    return (high_part * right % modulus * 256 + low_part * right) % modulus

def cos_sin(index, modulus):
    angle = index.astype(jnp.float32) * (TWO_PI / modulus)
    return (jnp.cos(angle), jnp.sin(angle))

def rounded(value):
    return lax.optimization_barrier(value.astype(jnp.bfloat16)).astype(jnp.float32)

def facet_terms(slab, window, offsets, position, scale):
    num_rows = slab.shape[0]
    facet_width = slab.shape[2]
    sub_count = offsets.shape[0]
    col_block = min(512, facet_width)
    freq = jnp.arange(SG, dtype=jnp.int32)
    inner = jnp.arange(col_block, dtype=jnp.int32)
    base_cos, base_sin = cos_sin(inner[:, None] * freq[None, :] % IMAGE, IMAGE)
    base_sin = -base_sin

    def one_block(block_idx, totals):
        first_col = block_idx * col_block
        cols = first_col + inner
        part_data = lax.dynamic_slice_in_dim(slab, first_col, col_block, 2).astype(jnp.float32)
        weights = lax.dynamic_slice_in_dim(window, first_col, col_block, 0)
        real_in = part_data[:, 0] * weights
        imag_in = part_data[:, 1] * weights
        cos_shift, sin_shift = cos_sin(offsets[:, None] * cols[None, :] % IMAGE, IMAGE)
        sin_shift = -sin_shift
        g_real = real_in[None] * cos_shift[:, None] - imag_in[None] * sin_shift[:, None]
        g_imag = real_in[None] * sin_shift[:, None] + imag_in[None] * cos_shift[:, None]
        g_real = rounded(g_real.reshape(sub_count * num_rows, col_block))
        g_imag = rounded(g_imag.reshape(sub_count * num_rows, col_block))
        phase_cos, phase_sin = cos_sin(first_col * freq % IMAGE, IMAGE)
        phase_sin = -phase_sin
        t_real = rounded(phase_cos[None] * base_cos - phase_sin[None] * base_sin)
        t_imag = rounded(phase_cos[None] * base_sin + phase_sin[None] * base_cos)
        high = lax.Precision.HIGHEST
        acc_real = totals[0] + jnp.dot(g_real, t_real, precision=high) - jnp.dot(g_imag, t_imag, precision=high)
        acc_imag = totals[1] + jnp.dot(g_real, t_imag, precision=high) + jnp.dot(g_imag, t_real, precision=high)
        return (acc_real, acc_imag)
    zero_sum = jnp.zeros((sub_count * num_rows, SG), jnp.float32)
    acc_real, acc_imag = lax.fori_loop(0, facet_width // col_block, one_block, (zero_sum, zero_sum))
    acc_real = acc_real.reshape(sub_count, num_rows, SG)
    acc_imag = acc_imag.reshape(sub_count, num_rows, SG)
    ratio = IMAGE // facet_width
    freq_all = (offsets[:, None] + freq[None, :]) % IMAGE
    cos_out, sin_out = cos_sin(position * (freq_all % ratio) % ratio, ratio)
    sin_out = -sin_out
    out_real = (acc_real * cos_out[:, None] - acc_imag * sin_out[:, None]) * scale
    out_imag = (acc_real * sin_out[:, None] + acc_imag * cos_out[:, None]) * scale
    return jnp.stack([out_real, out_imag], axis=2)

def row_terms(stripes, positions, rows_index, band_start, scale):
    shifted = (rows_index + band_start) % IMAGE
    cos_row, sin_row = cos_sin(mul_mod(positions[None, :], shifted[:, None], IMAGE), IMAGE)
    sin_row = -sin_row
    high = lax.Precision.HIGHEST
    first = jnp.einsum('jr,qrck->jqck', cos_row, stripes, precision=high)
    second = jnp.einsum('jr,qrck->jqck', sin_row, stripes, precision=high)
    real_part = first[:, :, 0] - second[:, :, 1]
    imag_part = first[:, :, 1] + second[:, :, 0]
    return jnp.stack([real_part, imag_part], axis=2) * scale

def sub_tables():
    freq = jnp.arange(SG, dtype=jnp.int32)
    out_block = min(512, SG)
    inner = jnp.arange(out_block, dtype=jnp.int32)
    base_cos, base_sin = cos_sin(freq[:, None] * inner[None, :] % SG, SG)
    cos_parts = []
    sin_parts = []
    for first_out in range(0, SG, out_block):
        phase_cos, phase_sin = cos_sin(freq * first_out % SG, SG)
        cos_parts.append(rounded(phase_cos[:, None] * base_cos - phase_sin[:, None] * base_sin))
        sin_parts.append(rounded(phase_cos[:, None] * base_sin + phase_sin[:, None] * base_cos))
    return (jnp.concatenate(cos_parts, axis=1), jnp.concatenate(sin_parts, axis=1))

def finish(rows_done, extents, t_cos, t_sin):
    freq = jnp.arange(SG, dtype=jnp.int32)
    keep = (freq >= extents[0]) & (freq < SG - extents[1])
    real_in = rounded(jnp.where(keep[None, :], rows_done[:, 0], jnp.float32(0.0)))
    imag_in = rounded(jnp.where(keep[None, :], rows_done[:, 1], jnp.float32(0.0)))
    high = lax.Precision.HIGHEST
    scale = 1.0 / math.sqrt(SG)
    real_out = (jnp.dot(real_in, t_cos, precision=high) - jnp.dot(imag_in, t_sin, precision=high)) * scale
    imag_out = (jnp.dot(real_in, t_sin, precision=high) + jnp.dot(imag_in, t_cos, precision=high)) * scale
    return jnp.stack([real_out, imag_out], axis=1)

def reference(facet_slab, window, facet_offsets, subgrid_offsets, row_positions, band_offset, mask_extents):
    scale_one = 1.0 / math.sqrt(FS * N_FACET)
    stripes = jnp.zeros((Q, ROWS_TOTAL, 2, SG), jnp.float32)
    for facet_idx in range(N_FACET):
        slab = facet_slab[:, :, facet_idx * FS:(facet_idx + 1) * FS]
        stripes = stripes + facet_terms(slab, window, subgrid_offsets, facet_offsets[facet_idx], scale_one)
    rows_index = jnp.arange(SGROWS, dtype=jnp.int32)
    rows_done = row_terms(stripes, row_positions, rows_index, band_offset[0], 1.0 / math.sqrt(ROWS_TOTAL))
    t_cos, t_sin = sub_tables()
    results = []
    for subgrid_idx in range(Q):
        results.append(finish(rows_done[:, subgrid_idx], mask_extents[subgrid_idx], t_cos, t_sin))
    return jnp.stack(results, axis=1)
```

```python
import math

import jax
import jax.numpy as jnp
from jax import lax
from jax.experimental import pallas as pl
from jax.experimental.pallas import tpu as pltpu
from jax.sharding import PartitionSpec as P

MESH = pl.DeviceIdType.MESH
F32 = jnp.float32
BF16 = jnp.bfloat16
NF = 8
NS = 16
ROWS = 256
XW = 512
NI = 256
SG = 2048


def cs(n):
    quad = (n + 8192) >> 14
    th = (n - (quad << 14)).astype(F32) * (2.0 * math.pi / 65536)
    t2 = th * th
    s = th * (1.0 + t2 * (-1.0 / 6 + t2 * (1.0 / 120 - t2 * (1.0 / 5040))))
    c = 1.0 + t2 * (-0.5 + t2 * (1.0 / 24 + t2 * (-1.0 / 720 + t2 * (1.0 / 40320))))
    odd = (quad & 1) == 1
    cos = jnp.where(odd, s, c)
    sin = jnp.where(odd, c, s)
    cos = jnp.where(((quad + 1) & 2) == 2, -cos, cos)
    sin = jnp.where((quad & 2) == 2, -sin, sin)
    return cos, sin


def iota(shape, dim):
    return lax.broadcasted_iota(jnp.int32, shape, dim)


def cmul(a, b):
    return a[0] * b[0] - a[1] * b[1], a[0] * b[1] + a[1] * b[0]


def cadd(a, b):
    return a[0] + b[0], a[1] + b[1]


def csub(a, b):
    return a[0] - b[0], a[1] - b[1]


def times_i(a):
    return -a[1], a[0]


def dft4(x0, x1, x2, x3):
    a, b = cadd(x0, x2), csub(x0, x2)
    c, d = cadd(x1, x3), times_i(csub(x1, x3))
    return cadd(a, c), cadd(b, d), csub(a, c), csub(b, d)


def dft8(t):
    even = dft4(t[0], t[2], t[4], t[6])
    odd = dft4(t[1], t[3], t[5], t[7])
    h = math.sqrt(0.5)
    o1 = ((odd[1][0] - odd[1][1]) * h, (odd[1][0] + odd[1][1]) * h)
    o2 = times_i(odd[2])
    o3 = ((-odd[3][0] - odd[3][1]) * h, (odd[3][0] - odd[3][1]) * h)
    odd = (odd[0], o1, o2, o3)
    return [cadd(e, o) for e, o in zip(even, odd)] + [csub(e, o) for e, o in zip(even, odd)]


def split(v):
    high = v.astype(BF16)
    return high, (v - high.astype(F32)).astype(BF16)


def kernel(
    d_ref, win_ref, pos_ref, fo_ref, so_ref, band_ref, ext_ref, out_ref,
    buf1, e_ref, send2, buf2, fb, send3, buf3, a_ref, w_ref, z_ref, send4, buf4, v_ref, tp_ref,
    s1, r1, s2, r2, s3, r3, s4, r4, loc,
):
    fi = lax.axis_index("facet")
    si = lax.axis_index("sub")
    m_own = si // 2
    jh = si % 2
    dest4 = 2 * fi + jh
    src4 = si // 2
    self4 = (fi == si // 2).astype(jnp.int32)

    barrier = pltpu.get_barrier_semaphore()

    def greet(f, s):
        pl.semaphore_signal(barrier, inc=1, device_id=(f, s), device_id_type=MESH)

    def greet_sub(k, c):
        greet(fi, (si + k) % NS)
        return c

    def greet_facet(k, c):
        greet((fi + k) % NF, si)
        return c

    def greet_last(m, c):
        @pl.when(jnp.logical_not(jnp.logical_and(src4 == fi, m == m_own)))
        def _():
            greet(src4, 2 * m + jh)

        return c

    lax.fori_loop(1, NS, greet_sub, 0)
    lax.fori_loop(1, NF, greet_facet, 0)
    lax.fori_loop(0, NF, greet_last, 0)
    pl.semaphore_wait(barrier, NS - 1 + NF - 1 + NF - self4)

    def copy1(k):
        to = (si + k) % NS
        return pltpu.make_async_remote_copy(
            src_ref=d_ref.at[:, :, pl.ds(pl.multiple_of(to * XW, XW), XW)],
            dst_ref=buf1.at[:, pl.ds(pl.multiple_of(si * 16, 16), 16), :],
            send_sem=s1.at[k], recv_sem=r1.at[k],
            device_id=(fi, to), device_id_type=MESH,
        )

    def go1(k, c):
        copy1(k).start()
        return c

    lax.fori_loop(1, NS, go1, 0)
    own1 = pltpu.make_async_copy(
        d_ref.at[:, :, pl.ds(pl.multiple_of(si * XW, XW), XW)],
        buf1.at[:, pl.ds(pl.multiple_of(si * 16, 16), 16), :],
        loc.at[0],
    )
    own1.start()

    band = band_ref[0]
    pos = pos_ref[...]

    def row_table(g, c):
        t = pos * (iota((8, ROWS), 0) + (8 * g + band))
        cos, sin = cs(t)
        for col, blk in ((0, (cos, -sin)), (1, (sin, cos))):
            high, low = split(jnp.concatenate(blk, axis=0))
            e_ref[0, pl.ds(pl.multiple_of(16 * g, 16), 16), pl.ds(col * ROWS, ROWS)] = high
            e_ref[1, pl.ds(pl.multiple_of(16 * g, 16), 16), pl.ds(col * ROWS, ROWS)] = low
        return c

    lax.fori_loop(0, 16, row_table, 0)

    lane = iota((1, 256), 1)
    off = jnp.zeros((1, 256), jnp.int32)
    for b in range(NF):
        off = jnp.where((lane >> 5) == b, fo_ref[b], off)

    def facet_table(g, c):
        row = iota((32, 256), 0)
        col = iota((32, 256), 1)
        cos, sin = cs(jnp.broadcast_to(off * (g * 8192), (32, 256)))
        rc, cc = (row >> 3) & 1, (col >> 3) & 1
        val = jnp.where(rc == cc, cos, jnp.where(rc == 0, sin, -sin))
        val = jnp.where(((row ^ col) & 0b10111) == 0, val, 0.0)
        fb[pl.ds(pl.multiple_of(32 * g, 32), 32), :] = val.astype(BF16)
        return c

    lax.fori_loop(0, NF, facet_table, 0)

    def first_freq(q):
        o = so_ref[q]
        return o + ((m_own - o) & 7)

    lane = iota((1, 128), 1)
    freq = jnp.zeros((1, 128), jnp.int32)
    for q in range(NF):
        freq = jnp.where(lane == q, first_freq(q), freq)

    def column_table(ac, c):
        step = 32
        a0 = ac * step
        base = cs((iota((step, NI), 0) + a0) * iota((step, NI), 1) * 8)
        ph = cs((iota((step, 128), 0) + a0) * freq)
        for q in range(NF):
            pq = (
                jnp.broadcast_to(ph[0][:, q : q + 1], (step, NI)),
                jnp.broadcast_to(ph[1][:, q : q + 1], (step, NI)),
            )
            cos, sin = cmul(base, pq)
            cos = cos.astype(BF16)
            sin = sin.astype(BF16)
            top = pl.ds(pl.multiple_of(a0, step), step)
            low = pl.ds(pl.multiple_of(a0 + XW, step), step)
            w_ref[q, top, pl.ds(0, NI)] = cos
            w_ref[q, top, pl.ds(NI, NI)] = -sin
            w_ref[q, low, pl.ds(0, NI)] = sin
            w_ref[q, low, pl.ds(NI, NI)] = cos
        return c

    lax.fori_loop(0, XW // 32, column_table, 0)

    fq = jnp.zeros((NF, NI), jnp.int32)
    for q in range(NF):
        fq = jnp.where(iota((NF, NI), 0) == q, first_freq(q), fq)
    fq = fq + 8 * iota((NF, NI), 1)
    z1 = cs(fq * 512)
    z2 = cs(fq * 1024)
    z_ref[0], z_ref[1] = z1[0], -z1[1]
    z_ref[2], z_ref[3] = z2[0], -z2[1]

    def sub_table(g, c):
        cos, sin = cs((iota((32, NI), 0) + 32 * g) * iota((32, NI), 1) * 256)
        at = pl.ds(pl.multiple_of(32 * g, 32), 32)
        for n, part in enumerate((cos, sin)):
            high, low = split(part)
            v_ref[0, at, pl.ds(n * NI, NI)] = high
            v_ref[1, at, pl.ds(n * NI, NI)] = low
        return c

    lax.fori_loop(0, 8, sub_table, 0)

    own1.wait()

    def wait1(k, c):
        pltpu.make_async_remote_copy(
            src_ref=d_ref.at[:, :, pl.ds(0, XW)],
            dst_ref=buf1.at[:, pl.ds(pl.multiple_of(((si - k + NS) % NS) * 16, 16), 16), :],
            send_sem=s1.at[k], recv_sem=r1.at[k],
            device_id=(fi, si), device_id_type=MESH,
        ).wait_recv()
        return c

    lax.fori_loop(1, NS, wait1, 0)

    data = buf1[...].reshape(2 * ROWS, XW)
    rows = jnp.dot(e_ref[0], data, preferred_element_type=F32) + jnp.dot(
        e_ref[1], data, preferred_element_type=F32
    )
    send2[...] = rows.astype(BF16).reshape(NF, 32, XW)

    def copy2(k):
        to = (fi + k) % NF
        return pltpu.make_async_remote_copy(
            src_ref=send2.at[to], dst_ref=buf2.at[fi],
            send_sem=s2.at[k], recv_sem=r2.at[k],
            device_id=(to, si), device_id_type=MESH,
        )

    def go2(k, c):
        copy2(k).start()
        return c

    lax.fori_loop(1, NF, go2, 0)
    own2 = pltpu.make_async_copy(send2.at[fi], buf2.at[fi], loc.at[1])
    own2.start()
    own2.wait()

    def wait2(k, c):
        pltpu.make_async_remote_copy(
            src_ref=send2.at[0], dst_ref=buf2.at[(fi - k + NF) % NF],
            send_sem=s2.at[k], recv_sem=r2.at[k],
            device_id=(fi, si), device_id_type=MESH,
        ).wait_recv()
        return c

    lax.fori_loop(1, NF, wait2, 0)

    win = win_ref[:, pl.ds(pl.multiple_of(si * XW, XW), XW)]
    summed = jnp.dot(fb[...], buf2[...].reshape(256, XW), preferred_element_type=F32)
    send3[...] = (summed * win).astype(BF16).reshape(NS, 16, XW)

    def copy3(k):
        to = (si + k) % NS
        return pltpu.make_async_remote_copy(
            src_ref=send3.at[to], dst_ref=buf3.at[si],
            send_sem=s3.at[k], recv_sem=r3.at[k],
            device_id=(fi, to), device_id_type=MESH,
        )

    def go3(k, c):
        copy3(k).start()
        return c

    lax.fori_loop(1, NS, go3, 0)
    own3 = pltpu.make_async_copy(send3.at[si], buf3.at[si], loc.at[2])
    own3.start()
    own3.wait()

    def wait3(k, c):
        pltpu.make_async_remote_copy(
            src_ref=send3.at[0], dst_ref=buf3.at[(si - k + NS) % NS],
            send_sem=s3.at[k], recv_sem=r3.at[k],
            device_id=(fi, si), device_id_type=MESH,
        ).wait_recv()
        return c

    lax.fori_loop(1, NS, wait3, 0)

    for t in range(8):
        one = buf3[2 * t].astype(F32)
        two = buf3[2 * t + 1].astype(F32)
        for c in range(2):
            part = jnp.concatenate([one[8 * c : 8 * c + 8], two[8 * c : 8 * c + 8]], axis=0)
            a_ref[pl.ds(16 * t, 16), pl.ds(c * XW, XW)] = part.astype(BF16)

    def copy4(q):
        return pltpu.make_async_remote_copy(
            src_ref=send4.at[q], dst_ref=buf4.at[m_own],
            send_sem=s4.at[q], recv_sem=r4.at[m_own],
            device_id=(q, dest4), device_id_type=MESH,
        )

    def own4():
        return pltpu.make_async_copy(send4.at[fi], buf4.at[m_own], loc.at[3])

    def columns(q, c):
        y = jnp.dot(a_ref[...], w_ref[q], preferred_element_type=F32)

        def part(e):
            return y[8 * e : 8 * e + 8, :NI], y[8 * e : 8 * e + 8, NI:]

        def row(n):
            return jnp.broadcast_to(z_ref[n, pl.ds(q, 1), :], (8, NI))

        zz = (row(2), row(3))
        even, odd = part(14), part(15)
        for e in range(12, -1, -2):
            even = cadd(cmul(even, zz), part(e))
            odd = cadd(cmul(odd, zz), part(e + 1))
        total = cadd(even, cmul(odd, (row(0), row(1))))
        k = ((m_own - so_ref[q]) & 7) + 8 * iota((8, NI), 1)
        keep = jnp.logical_and(k >= ext_ref[q, 0], k < SG - ext_ref[q, 1])
        both = jnp.concatenate(
            [jnp.where(keep, total[0], 0.0), jnp.where(keep, total[1], 0.0)], axis=0
        )
        send4[q] = both.astype(BF16)
        mine = jnp.logical_and(q == fi, dest4 == si)

        @pl.when(mine)
        def _():
            own4().start()

        @pl.when(jnp.logical_not(mine))
        def _():
            copy4(q).start()

        return c

    lax.fori_loop(0, NF, columns, 0)

    def wait4(m, c):
        mine = jnp.logical_and(src4 == fi, m == m_own)

        @pl.when(mine)
        def _():
            own4().wait()

        @pl.when(jnp.logical_not(mine))
        def _():
            pltpu.make_async_remote_copy(
                src_ref=send4.at[0], dst_ref=buf4.at[m],
                send_sem=s4.at[0], recv_sem=r4.at[m],
                device_id=(fi, si), device_id_type=MESH,
            ).wait_recv()

        return c

    tw = cs(iota((NF, NI), 0) * iota((NF, NI), 1) * 32)
    lax.fori_loop(0, NF, wait4, 0)

    got = buf4[...].reshape(128, NI)
    spec = jnp.dot(got, v_ref[0], preferred_element_type=F32) + jnp.dot(
        got, v_ref[1], preferred_element_type=F32
    )
    for m in range(NF):
        re, im = spec[16 * m : 16 * m + 8], spec[16 * m + 8 : 16 * m + 16]
        tp_ref[m, 0] = re[:, :NI] - im[:, NI:]
        tp_ref[m, 1] = re[:, NI:] + im[:, :NI]
    own = so_ref[fi]
    terms = []
    for kap in range(NF):
        got = tp_ref[(own + kap) & 7]
        step = (
            jnp.broadcast_to(tw[0][kap : kap + 1], (8, NI)),
            jnp.broadcast_to(tw[1][kap : kap + 1], (8, NI)),
        )
        terms.append(cmul((got[0], got[1]), step))
    scale = 1.0 / (4096.0 * math.sqrt(SG))
    for n, val in enumerate(dft8(terms)):
        out_ref[0, :, pl.ds(n * NI, NI)] = val[0] * scale
        out_ref[1, :, pl.ds(n * NI, NI)] = val[1] * scale

    def done1(k, c):
        copy1(k).wait_send()
        copy3(k).wait_send()
        return c

    def done2(k, c):
        copy2(k).wait_send()
        return c

    def done4(q, c):
        @pl.when(jnp.logical_not(jnp.logical_and(q == fi, dest4 == si)))
        def _():
            copy4(q).wait_send()

        return c

    lax.fori_loop(1, NS, done1, 0)
    lax.fori_loop(1, NF, done2, 0)
    lax.fori_loop(0, NF, done4, 0)


def local(slab, window, facet_offsets, subgrid_offsets, row_positions, band_offset, extents):
    vmem = pl.BlockSpec(memory_space=pltpu.VMEM)
    smem = pl.BlockSpec(memory_space=pltpu.SMEM)
    dma = pltpu.SemaphoreType.DMA
    out = pl.pallas_call(
        kernel,
        out_shape=jax.ShapeDtypeStruct((2, 8, SG), F32),
        in_specs=[pl.BlockSpec(memory_space=pl.ANY), vmem, vmem, smem, smem, smem, smem],
        out_specs=vmem,
        scratch_shapes=[
            pltpu.VMEM((2, ROWS, XW), BF16),
            pltpu.VMEM((2, ROWS, 2 * ROWS), BF16),
            pltpu.VMEM((NF, 32, XW), BF16),
            pltpu.VMEM((NF, 32, XW), BF16),
            pltpu.VMEM((256, 256), BF16),
            pltpu.VMEM((NS, 16, XW), BF16),
            pltpu.VMEM((NS, 16, XW), BF16),
            pltpu.VMEM((128, 2 * XW), BF16),
            pltpu.VMEM((NF, 2 * XW, 2 * NI), BF16),
            pltpu.VMEM((4, NF, NI), F32),
            pltpu.VMEM((NF, 16, NI), BF16),
            pltpu.VMEM((NF, 16, NI), BF16),
            pltpu.VMEM((2, NI, 2 * NI), BF16),
            pltpu.VMEM((NF, 2, 8, NI), F32),
            dma((NS,)), dma((NS,)), dma((NF,)), dma((NF,)),
            dma((NS,)), dma((NS,)), dma((NF,)), dma((NF,)), dma((4,)),
        ],
        compiler_params=pltpu.CompilerParams(
            collective_id=0, has_side_effects=True, vmem_limit_bytes=40 << 20
        ),
    )(
        slab.transpose(1, 0, 2), window.reshape(1, -1), row_positions.reshape(1, -1),
        facet_offsets, subgrid_offsets, band_offset, extents,
    )
    return out.transpose(1, 0, 2)[:, None]


def solution(mesh):
    return jax.shard_map(
        local,
        mesh=mesh,
        in_specs=(P("sub", None, "facet"), P(), P(), P(), P(), P(), P()),
        out_specs=P("sub", "facet", None, None),
        check_vma=False,
    )
```

```python
import math

import jax
import jax.numpy as jnp
from jax import lax
from jax.experimental import pallas as pl
from jax.experimental.pallas import tpu as pltpu
from jax.sharding import PartitionSpec as P

MESH = pl.DeviceIdType.MESH
F32 = jnp.float32
BF16 = jnp.bfloat16
NF = 8
NS = 16
ROWS = 256
XW = 512
NI = 256
SG = 2048
C = 4
CW = XW // C
ORDER = tuple((step, ch) for step in "rfg" for ch in range(C))


def cs(n):
    quad = (n + 8192) >> 14
    th = (n - (quad << 14)).astype(F32) * (2.0 * math.pi / 65536)
    t2 = th * th
    s = th * (1.0 + t2 * (-1.0 / 6 + t2 * (1.0 / 120 - t2 * (1.0 / 5040))))
    c = 1.0 + t2 * (-0.5 + t2 * (1.0 / 24 + t2 * (-1.0 / 720 + t2 * (1.0 / 40320))))
    odd = (quad & 1) == 1
    cos = jnp.where(odd, s, c)
    sin = jnp.where(odd, c, s)
    cos = jnp.where(((quad + 1) & 2) == 2, -cos, cos)
    sin = jnp.where((quad & 2) == 2, -sin, sin)
    return cos, sin


def iota(shape, dim):
    return lax.broadcasted_iota(jnp.int32, shape, dim)


def cmul(a, b):
    return a[0] * b[0] - a[1] * b[1], a[0] * b[1] + a[1] * b[0]


def cadd(a, b):
    return a[0] + b[0], a[1] + b[1]


def csub(a, b):
    return a[0] - b[0], a[1] - b[1]


def times_i(a):
    return -a[1], a[0]


def dft4(x0, x1, x2, x3):
    a, b = cadd(x0, x2), csub(x0, x2)
    c, d = cadd(x1, x3), times_i(csub(x1, x3))
    return cadd(a, c), cadd(b, d), csub(a, c), csub(b, d)


def dft8(t):
    even = dft4(t[0], t[2], t[4], t[6])
    odd = dft4(t[1], t[3], t[5], t[7])
    h = math.sqrt(0.5)
    o1 = ((odd[1][0] - odd[1][1]) * h, (odd[1][0] + odd[1][1]) * h)
    o2 = times_i(odd[2])
    o3 = ((-odd[3][0] - odd[3][1]) * h, (odd[3][0] - odd[3][1]) * h)
    odd = (odd[0], o1, o2, o3)
    return [cadd(e, o) for e, o in zip(even, odd)] + [csub(e, o) for e, o in zip(even, odd)]


def split(v):
    high = v.astype(BF16)
    return high, (v - high.astype(F32)).astype(BF16)


def kernel(
    d_ref, win_hbm, pos_hbm, fo_hbm, so_hbm, band_hbm, ext_hbm, out_ref,
    win_ref, pos_ref, fo_ref, so_ref, band_ref, ext_ref,
    buf1, e_ref, send2, buf2, fb, send3, buf3, a_ref, w_ref, z_ref, send4, buf4, v_ref, tp_ref,
    sends, r1, r2, r3, r4, loc, small,
):
    fi = lax.axis_index("facet")
    si = lax.axis_index("sub")
    m_own = si >> 1
    jh = si & 1
    dest4 = 2 * fi + jh
    src4 = si >> 1
    is_own4 = fi == src4

    smalls = [
        pltpu.make_async_copy(src, dst, small.at[n])
        for n, (src, dst) in enumerate((
            (pos_hbm, pos_ref), (band_hbm, band_ref), (fo_hbm, fo_ref), (so_hbm, so_ref),
            (ext_hbm, ext_ref),
            (win_hbm.at[:, pl.ds(pl.multiple_of(si * XW, XW), XW)], win_ref),
        ))
    ]
    for copy in smalls:
        copy.start()
    slab = d_ref.reshape(32, d_ref.shape[2])

    def own1(ch):
        return pltpu.make_async_copy(
            slab.at[:, pl.ds(pl.multiple_of(si * XW + ch * CW, CW), CW)],
            buf1.at[ch, pl.ds(pl.multiple_of(si * 32, 32), 32), :],
            loc.at[ch],
        )

    for ch in range(C):
        own1(ch).start()

    barrier = pltpu.get_barrier_semaphore()

    def greet(f, s):
        pl.semaphore_signal(barrier, inc=1, device_id=(f, s), device_id_type=MESH)

    def greet_sub(k, c):
        greet(fi, (si + k) & (NS - 1))
        return c

    def greet_facet(k, c):
        greet((fi + k) & (NF - 1), si)
        return c

    def greet_last(m, c):
        @pl.when(jnp.logical_not(jnp.logical_and(is_own4, m == m_own)))
        def _():
            greet(src4, 2 * m + jh)

        return c

    lax.fori_loop(1, NS, greet_sub, 0)
    lax.fori_loop(1, NF, greet_facet, 0)
    lax.fori_loop(0, NF, greet_last, 0)
    pl.semaphore_wait(barrier, NS - 1 + NF - 1 + NF - is_own4.astype(jnp.int32))

    for ch in range(C):

        def go1(k, c, ch=ch):
            to = (si + k) & (NS - 1)
            pltpu.make_async_remote_copy(
                src_ref=slab.at[:, pl.ds(pl.multiple_of(to * XW + ch * CW, CW), CW)],
                dst_ref=buf1.at[ch, pl.ds(pl.multiple_of(si * 32, 32), 32), :],
                send_sem=sends.at[0], recv_sem=r1.at[ch],
                device_id=(fi, to), device_id_type=MESH,
            ).start()
            return c

        lax.fori_loop(1, NS, go1, 0)

    for copy in smalls:
        copy.wait()

    band = band_ref[0]
    pos = pos_ref[...]
    pick = (iota((ROWS, 2 * ROWS), 1) >> 1 == iota((ROWS, 2 * ROWS), 0)).astype(BF16)
    digits = jnp.concatenate([pos >> 8, pos & 255], axis=0).astype(F32).astype(BF16)
    digits = jnp.dot(digits, pick, preferred_element_type=F32).astype(jnp.int32)
    twice = digits[0:1] * 256 + digits[1:2]
    turn = (iota((1, 2 * ROWS), 1) & 1) * 16384

    def row_table(g, c):
        cos, sin = cs(twice * (iota((8, 2 * ROWS), 0) + (8 * g + band)) - turn)
        high, low = split(jnp.concatenate([cos, -sin], axis=0))
        at = pl.ds(pl.multiple_of(16 * g, 16), 16)
        e_ref[0, at, :] = high
        e_ref[1, at, :] = low
        return c

    lax.fori_loop(0, 16, row_table, 0)

    lane = iota((1, 256), 1)
    off = jnp.zeros((1, 256), jnp.int32)
    for b in range(NF):
        off = jnp.where((lane >> 5) == b, fo_ref[b], off)

    def facet_table(g, c):
        row = iota((32, 256), 0)
        col = iota((32, 256), 1)
        cos, sin = cs(jnp.broadcast_to(off * (g * 8192), (32, 256)))
        rc, cc = (row >> 3) & 1, (col >> 3) & 1
        val = jnp.where(rc == cc, cos, jnp.where(rc == 0, sin, -sin))
        val = jnp.where(((row ^ col) & 0b10111) == 0, val, 0.0)
        fb[pl.ds(pl.multiple_of(32 * g, 32), 32), :] = val.astype(BF16)
        return c

    lax.fori_loop(0, NF, facet_table, 0)

    def first_freq(q):
        o = so_ref[q]
        return o + ((m_own - o) & 7)

    lane = iota((1, 128), 1)
    freq = jnp.zeros((1, 128), jnp.int32)
    for q in range(NF):
        freq = jnp.where(lane == q, first_freq(q), freq)

    def column_table(ac, c):
        step = 32
        a0 = ac * step
        base = cs((iota((step, NI), 0) + a0) * iota((step, NI), 1) * 8)
        ph = cs((iota((step, 128), 0) + a0) * freq)
        row = (ac // (CW // step)) * (2 * CW) + (ac % (CW // step)) * step
        top = pl.ds(pl.multiple_of(row, step), step)
        low = pl.ds(pl.multiple_of(row + CW, step), step)
        for q in range(NF):
            pq = (
                jnp.broadcast_to(ph[0][:, q : q + 1], (step, NI)),
                jnp.broadcast_to(ph[1][:, q : q + 1], (step, NI)),
            )
            cos, sin = cmul(base, pq)
            cos = cos.astype(BF16)
            sin = sin.astype(BF16)
            w_ref[q, top, pl.ds(0, NI)] = cos
            w_ref[q, top, pl.ds(NI, NI)] = -sin
            w_ref[q, low, pl.ds(0, NI)] = sin
            w_ref[q, low, pl.ds(NI, NI)] = cos
        return c

    lax.fori_loop(0, XW // 32, column_table, 0)

    fq = jnp.zeros((NF, NI), jnp.int32)
    for q in range(NF):
        fq = jnp.where(iota((NF, NI), 0) == q, first_freq(q), fq)
    fq = fq + 8 * iota((NF, NI), 1)
    z1 = cs(fq * 512)
    z2 = cs(fq * 1024)
    z_ref[0], z_ref[1] = z1[0], -z1[1]
    z_ref[2], z_ref[3] = z2[0], -z2[1]

    def sub_table(g, c):
        cos, sin = cs((iota((32, NI), 0) + 32 * g) * iota((32, NI), 1) * 256)
        at = pl.ds(pl.multiple_of(32 * g, 32), 32)
        for n, part in enumerate((cos, sin)):
            high, low = split(part)
            v_ref[0, at, pl.ds(n * NI, NI)] = high
            v_ref[1, at, pl.ds(n * NI, NI)] = low
        return c

    lax.fori_loop(0, 8, sub_table, 0)

    def wait(ref, sem):
        pltpu.make_async_copy(ref, ref, sem).wait()

    def rows(ch):
        own1(ch).wait()
        wait(buf1.at[ch, pl.ds(0, 480), :], r1.at[ch])
        data = buf1[ch]
        val = jnp.dot(e_ref[0], data, preferred_element_type=F32) + jnp.dot(
            e_ref[1], data, preferred_element_type=F32
        )
        send2[ch] = val.astype(BF16).reshape(NF, 32, CW)

        def go2(k, c):
            to = (fi + k) & (NF - 1)
            pltpu.make_async_remote_copy(
                src_ref=send2.at[ch, to], dst_ref=buf2.at[ch, fi],
                send_sem=sends.at[1], recv_sem=r2.at[ch],
                device_id=(to, si), device_id_type=MESH,
            ).start()
            return c

        lax.fori_loop(1, NF, go2, 0)
        buf2[ch, fi] = send2[ch, fi]

    def facets(ch):
        wait(buf2.at[ch, pl.ds(0, NF - 1)], r2.at[ch])
        summed = jnp.dot(fb[...], buf2[ch].reshape(256, CW), preferred_element_type=F32)
        val = summed * win_ref[:, pl.ds(ch * CW, CW)]
        send3[ch] = val.astype(BF16).reshape(NS, 16, CW)

        def go3(k, c):
            to = (si + k) & (NS - 1)
            pltpu.make_async_remote_copy(
                src_ref=send3.at[ch, to], dst_ref=buf3.at[ch, si],
                send_sem=sends.at[2], recv_sem=r3.at[ch],
                device_id=(fi, to), device_id_type=MESH,
            ).start()
            return c

        lax.fori_loop(1, NS, go3, 0)
        buf3[ch, si] = send3[ch, si]

    def gather(ch):
        wait(buf3.at[ch, pl.ds(0, NS - 1)], r3.at[ch])
        for t in range(8):
            one = buf3[ch, 2 * t].astype(F32)
            two = buf3[ch, 2 * t + 1].astype(F32)
            for c in range(2):
                part = jnp.concatenate([one[8 * c : 8 * c + 8], two[8 * c : 8 * c + 8]], axis=0)
                a_ref[pl.ds(16 * t, 16), pl.ds((2 * ch + c) * CW, CW)] = part.astype(BF16)

    steps = {"r": rows, "f": facets, "g": gather}
    for name, ch in ORDER:
        steps[name](ch)

    def copy4(q):
        return pltpu.make_async_remote_copy(
            src_ref=send4.at[q], dst_ref=buf4.at[m_own],
            send_sem=sends.at[3], recv_sem=r4,
            device_id=(q, dest4), device_id_type=MESH,
        )

    for n in range(NF):
        q = (fi + 1 + n) & (NF - 1)
        y = jnp.dot(a_ref[...], w_ref[q], preferred_element_type=F32)

        def part(e):
            return y[8 * e : 8 * e + 8, :NI], y[8 * e : 8 * e + 8, NI:]

        def row(i):
            return jnp.broadcast_to(z_ref[i, pl.ds(q, 1), :], (8, NI))

        zz = (row(2), row(3))
        even, odd = part(14), part(15)
        for e in range(12, -1, -2):
            even = cadd(cmul(even, zz), part(e))
            odd = cadd(cmul(odd, zz), part(e + 1))
        total = cadd(even, cmul(odd, (row(0), row(1))))
        k = ((m_own - so_ref[q]) & 7) + 8 * iota((8, NI), 1)
        keep = jnp.logical_and(k >= ext_ref[0, q], k < SG - ext_ref[1, q])
        both = jnp.concatenate(
            [jnp.where(keep, total[0], 0.0), jnp.where(keep, total[1], 0.0)], axis=0
        )
        send4[q] = both.astype(BF16)
        if n < NF - 1:
            copy4(q).start()
        else:
            @pl.when(is_own4)
            def _():
                buf4[m_own] = send4[q]

            @pl.when(jnp.logical_not(is_own4))
            def _():
                copy4(q).start()

    tw = cs(iota((NF, NI), 0) * iota((NF, NI), 1) * 32)
    wait(buf1.at[:, pl.ds(0, 480), :], sends.at[0])
    wait(buf2.at[:, pl.ds(0, NF - 1)], sends.at[1])
    wait(buf3.at[:, pl.ds(0, NS - 1)], sends.at[2])

    @pl.when(is_own4)
    def _():
        wait(buf4.at[pl.ds(0, NF - 1)], r4)

    @pl.when(jnp.logical_not(is_own4))
    def _():
        wait(buf4, r4)

    got = buf4[...].reshape(128, NI)
    spec = jnp.dot(got, v_ref[0], preferred_element_type=F32) + jnp.dot(
        got, v_ref[1], preferred_element_type=F32
    )
    for m in range(NF):
        re, im = spec[16 * m : 16 * m + 8], spec[16 * m + 8 : 16 * m + 16]
        tp_ref[m, 0] = re[:, :NI] - im[:, NI:]
        tp_ref[m, 1] = re[:, NI:] + im[:, :NI]
    own = so_ref[fi]
    terms = []
    for kap in range(NF):
        got = tp_ref[(own + kap) & 7]
        step = (
            jnp.broadcast_to(tw[0][kap : kap + 1], (8, NI)),
            jnp.broadcast_to(tw[1][kap : kap + 1], (8, NI)),
        )
        terms.append(cmul((got[0], got[1]), step))
    scale = 1.0 / (4096.0 * math.sqrt(SG))
    for n, val in enumerate(dft8(terms)):
        out_ref[0, :, pl.ds(n * NI, NI)] = val[0] * scale
        out_ref[1, :, pl.ds(n * NI, NI)] = val[1] * scale

    @pl.when(is_own4)
    def _():
        wait(buf4.at[pl.ds(0, NF - 1)], sends.at[3])

    @pl.when(jnp.logical_not(is_own4))
    def _():
        wait(buf4, sends.at[3])


def local(slab, window, facet_offsets, subgrid_offsets, row_positions, band_offset, extents):
    hbm = pl.BlockSpec(memory_space=pltpu.MemorySpace.HBM)
    dma = pltpu.SemaphoreType.DMA
    out = pl.pallas_call(
        kernel,
        out_shape=jax.ShapeDtypeStruct((2, 8, SG), F32),
        in_specs=[hbm] * 7,
        out_specs=pl.BlockSpec(memory_space=pltpu.VMEM),
        scratch_shapes=[
            pltpu.VMEM((1, XW), F32),
            pltpu.VMEM((1, ROWS), jnp.int32),
            pltpu.SMEM((NF,), jnp.int32),
            pltpu.SMEM((NF,), jnp.int32),
            pltpu.SMEM((1,), jnp.int32),
            pltpu.SMEM((2, NF), jnp.int32),
            pltpu.VMEM((C, 2 * ROWS, CW), BF16),
            pltpu.VMEM((2, ROWS, 2 * ROWS), BF16),
            pltpu.VMEM((C, NF, 32, CW), BF16),
            pltpu.VMEM((C, NF, 32, CW), BF16),
            pltpu.VMEM((256, 256), BF16),
            pltpu.VMEM((C, NS, 16, CW), BF16),
            pltpu.VMEM((C, NS, 16, CW), BF16),
            pltpu.VMEM((128, 2 * XW), BF16),
            pltpu.VMEM((NF, 2 * XW, 2 * NI), BF16),
            pltpu.VMEM((4, NF, NI), F32),
            pltpu.VMEM((NF, 16, NI), BF16),
            pltpu.VMEM((NF, 16, NI), BF16),
            pltpu.VMEM((2, NI, 2 * NI), BF16),
            pltpu.VMEM((NF, 2, 8, NI), F32),
            dma((4,)), dma((C,)), dma((C,)), dma((C,)), dma, dma((C,)), dma((6,)),
        ],
        compiler_params=pltpu.CompilerParams(
            collective_id=0, has_side_effects=True, vmem_limit_bytes=63 << 20
        ),
    )(
        slab, window.reshape(1, -1), row_positions.reshape(1, -1),
        facet_offsets, subgrid_offsets, band_offset, extents.T,
    )
    return out.transpose(1, 0, 2)[:, None]


def solution(mesh):
    return jax.shard_map(
        local,
        mesh=mesh,
        in_specs=(P("sub", None, "facet"), P(), P(), P(), P(), P(), P()),
        out_specs=P("sub", "facet", None, None),
        check_vma=False,
    )
```

```python
import math

import jax
import jax.numpy as jnp
from jax import lax
from jax.experimental import pallas as pl
from jax.experimental.pallas import tpu as pltpu
from jax.sharding import PartitionSpec as P

MESH = pl.DeviceIdType.MESH
F32 = jnp.float32
BF16 = jnp.bfloat16
NF = 8
NS = 16
ROWS = 256
XW = 512
NI = 256
SG = 2048
C = 4
CW = XW // C
FAR = (True, True, True)
ORDER = tuple((step, ch) for step in "rfg" for ch in range(C))


def cs(n):
    quad = (n + 8192) >> 14
    th = (n - (quad << 14)).astype(F32) * (2.0 * math.pi / 65536)
    t2 = th * th
    s = th * (1.0 + t2 * (-1.0 / 6 + t2 * (1.0 / 120 - t2 * (1.0 / 5040))))
    c = 1.0 + t2 * (-0.5 + t2 * (1.0 / 24 + t2 * (-1.0 / 720 + t2 * (1.0 / 40320))))
    odd = (quad & 1) == 1
    cos = jnp.where(odd, s, c)
    sin = jnp.where(odd, c, s)
    cos = jnp.where(((quad + 1) & 2) == 2, -cos, cos)
    sin = jnp.where((quad & 2) == 2, -sin, sin)
    return cos, sin


def iota(shape, dim):
    return lax.broadcasted_iota(jnp.int32, shape, dim)


def cmul(a, b):
    return a[0] * b[0] - a[1] * b[1], a[0] * b[1] + a[1] * b[0]


def cadd(a, b):
    return a[0] + b[0], a[1] + b[1]


def csub(a, b):
    return a[0] - b[0], a[1] - b[1]


def times_i(a):
    return -a[1], a[0]


def dft4(x0, x1, x2, x3):
    a, b = cadd(x0, x2), csub(x0, x2)
    c, d = cadd(x1, x3), times_i(csub(x1, x3))
    return cadd(a, c), cadd(b, d), csub(a, c), csub(b, d)


def dft8(t):
    even = dft4(t[0], t[2], t[4], t[6])
    odd = dft4(t[1], t[3], t[5], t[7])
    h = math.sqrt(0.5)
    o1 = ((odd[1][0] - odd[1][1]) * h, (odd[1][0] + odd[1][1]) * h)
    o2 = times_i(odd[2])
    o3 = ((-odd[3][0] - odd[3][1]) * h, (odd[3][0] - odd[3][1]) * h)
    odd = (odd[0], o1, o2, o3)
    return [cadd(e, o) for e, o in zip(even, odd)] + [csub(e, o) for e, o in zip(even, odd)]


def split(v):
    high = v.astype(BF16)
    return high, (v - high.astype(F32)).astype(BF16)


def kernel(
    d_ref, win_hbm, pos_hbm, fo_hbm, so_hbm, band_hbm, ext_hbm, out_ref,
    win_ref, pos_ref, fo_ref, so_ref, band_ref, ext_ref,
    buf1, e_ref, send2, buf2, fb, send3, buf3, a_ref, w_ref, z_ref, send4, buf4, v_ref, tp_ref,
    sends, r1, r2, r3, r4, loc, small, near, far,
):
    fi = lax.axis_index("facet")
    si = lax.axis_index("sub")
    m_own = si >> 1
    jh = si & 1
    dest4 = 2 * fi + jh
    src4 = si >> 1
    is_own4 = fi == src4

    def sub_at(k):
        code = k >> 2
        x = ((si >> 1) + (code ^ (code >> 1))) & 3
        return ((si >> 3) ^ ((k >> 1) & 1)) * 8 + x * 2 + ((si & 1) ^ (k & 1))

    def facet_at(k):
        code = k >> 1
        return (((fi >> 1) + (code ^ (code >> 1))) & 3) * 2 + ((fi & 1) ^ (k & 1))

    beside = (((fi + 2) & 7, si), ((fi + 6) & 7, si), (fi ^ 1, si))
    barrier = pltpu.get_barrier_semaphore()

    def greet(k, c):
        to = sub_at(NS - k)
        pl.semaphore_signal(barrier, inc=1, device_id=(fi, to), device_id_type=MESH)
        return c

    for to in beside:
        pl.semaphore_signal(barrier, inc=1, device_id=to, device_id_type=MESH)
    lax.fori_loop(1, NS, greet, 0)

    smalls = [
        pltpu.make_async_copy(src, dst, small.at[n])
        for n, (src, dst) in enumerate((
            (pos_hbm, pos_ref), (band_hbm, band_ref), (fo_hbm, fo_ref), (so_hbm, so_ref),
            (ext_hbm, ext_ref),
            (win_hbm.at[:, pl.ds(pl.multiple_of(si * XW, XW), XW)], win_ref),
        ))
    ]
    for copy in smalls:
        copy.start()
    slab = d_ref.reshape(32, d_ref.shape[2])

    def own1(ch):
        return pltpu.make_async_copy(
            slab.at[:, pl.ds(pl.multiple_of(si * XW + ch * CW, CW), CW)],
            buf1.at[ch, pl.ds(pl.multiple_of(si * 32, 32), 32), :],
            loc.at[ch],
        )

    for ch in range(C):
        own1(ch).start()

    pl.semaphore_wait(barrier, NS - 1 + 3)

    for ch in range(C):

        def go1(k, c, ch=ch):
            to = sub_at(NS - k if FAR[0] else k)
            pltpu.make_async_remote_copy(
                src_ref=slab.at[:, pl.ds(pl.multiple_of(to * XW + ch * CW, CW), CW)],
                dst_ref=buf1.at[ch, pl.ds(pl.multiple_of(si * 32, 32), 32), :],
                send_sem=sends.at[0], recv_sem=r1.at[ch],
                device_id=(fi, to), device_id_type=MESH,
            ).start()
            return c

        lax.fori_loop(1, NS, go1, 0)

    for to in beside:
        pl.semaphore_signal(near, inc=1, device_id=to, device_id_type=MESH)

    for copy in smalls:
        copy.wait()

    band = band_ref[0]
    pos = pos_ref[...]
    pick = (iota((ROWS, 2 * ROWS), 1) >> 1 == iota((ROWS, 2 * ROWS), 0)).astype(BF16)
    digits = jnp.concatenate([pos >> 8, pos & 255], axis=0).astype(F32).astype(BF16)
    digits = jnp.dot(digits, pick, preferred_element_type=F32).astype(jnp.int32)
    twice = digits[0:1] * 256 + digits[1:2]
    turn = (iota((1, 2 * ROWS), 1) & 1) * 16384

    def row_table(g, c):
        cos, sin = cs(twice * (iota((8, 2 * ROWS), 0) + (8 * g + band)) - turn)
        high, low = split(jnp.concatenate([cos, -sin], axis=0))
        at = pl.ds(pl.multiple_of(16 * g, 16), 16)
        e_ref[0, at, :] = high
        e_ref[1, at, :] = low
        return c

    lax.fori_loop(0, 16, row_table, 0)

    lane = iota((1, 256), 1)
    off = jnp.zeros((1, 256), jnp.int32)
    for b in range(NF):
        off = jnp.where((lane >> 5) == b, fo_ref[b], off)

    def facet_table(g, c):
        row = iota((32, 256), 0)
        col = iota((32, 256), 1)
        cos, sin = cs(jnp.broadcast_to(off * (g * 8192), (32, 256)))
        rc, cc = (row >> 3) & 1, (col >> 3) & 1
        val = jnp.where(rc == cc, cos, jnp.where(rc == 0, sin, -sin))
        val = jnp.where(((row ^ col) & 0b10111) == 0, val, 0.0)
        fb[pl.ds(pl.multiple_of(32 * g, 32), 32), :] = val.astype(BF16)
        return c

    lax.fori_loop(0, NF, facet_table, 0)

    pl.semaphore_wait(near, 3)
    pl.semaphore_signal(far, inc=1, device_id=beside[1], device_id_type=MESH)

    def first_freq(q):
        o = so_ref[q]
        return o + ((m_own - o) & 7)

    lane = iota((1, 128), 1)
    freq = jnp.zeros((1, 128), jnp.int32)
    for q in range(NF):
        freq = jnp.where(lane == q, first_freq(q), freq)

    def column_table(ac, c):
        step = 32
        a0 = ac * step
        base = cs((iota((step, NI), 0) + a0) * iota((step, NI), 1) * 8)
        ph = cs((iota((step, 128), 0) + a0) * freq)
        row = (ac // (CW // step)) * (2 * CW) + (ac % (CW // step)) * step
        top = pl.ds(pl.multiple_of(row, step), step)
        low = pl.ds(pl.multiple_of(row + CW, step), step)
        for q in range(NF):
            pq = (
                jnp.broadcast_to(ph[0][:, q : q + 1], (step, NI)),
                jnp.broadcast_to(ph[1][:, q : q + 1], (step, NI)),
            )
            cos, sin = cmul(base, pq)
            cos = cos.astype(BF16)
            sin = sin.astype(BF16)
            w_ref[q, top, pl.ds(0, NI)] = cos
            w_ref[q, top, pl.ds(NI, NI)] = -sin
            w_ref[q, low, pl.ds(0, NI)] = sin
            w_ref[q, low, pl.ds(NI, NI)] = cos
        return c

    lax.fori_loop(0, XW // 32, column_table, 0)

    fq = jnp.zeros((NF, NI), jnp.int32)
    for q in range(NF):
        fq = jnp.where(iota((NF, NI), 0) == q, first_freq(q), fq)
    fq = fq + 8 * iota((NF, NI), 1)
    z1 = cs(fq * 512)
    z2 = cs(fq * 1024)
    z_ref[0], z_ref[1] = z1[0], -z1[1]
    z_ref[2], z_ref[3] = z2[0], -z2[1]

    def sub_table(g, c):
        cos, sin = cs((iota((32, NI), 0) + 32 * g) * iota((32, NI), 1) * 256)
        at = pl.ds(pl.multiple_of(32 * g, 32), 32)
        for n, part in enumerate((cos, sin)):
            high, low = split(part)
            v_ref[0, at, pl.ds(n * NI, NI)] = high
            v_ref[1, at, pl.ds(n * NI, NI)] = low
        return c

    lax.fori_loop(0, 8, sub_table, 0)
    pl.semaphore_wait(far, 1)

    def wait(ref, sem):
        pltpu.make_async_copy(ref, ref, sem).wait()

    def rows(ch):
        own1(ch).wait()
        wait(buf1.at[ch, pl.ds(0, 480), :], r1.at[ch])
        data = buf1[ch]
        val = jnp.dot(e_ref[0], data, preferred_element_type=F32) + jnp.dot(
            e_ref[1], data, preferred_element_type=F32
        )
        send2[ch] = val.astype(BF16).reshape(NF, 32, CW)

        def go2(k, c):
            to = facet_at(NF - k if FAR[1] else k)
            pltpu.make_async_remote_copy(
                src_ref=send2.at[ch, to], dst_ref=buf2.at[ch, fi],
                send_sem=sends.at[1], recv_sem=r2.at[ch],
                device_id=(to, si), device_id_type=MESH,
            ).start()
            return c

        lax.fori_loop(1, NF, go2, 0)
        buf2[ch, fi] = send2[ch, fi]

    def facets(ch):
        wait(buf2.at[ch, pl.ds(0, NF - 1)], r2.at[ch])
        summed = jnp.dot(fb[...], buf2[ch].reshape(256, CW), preferred_element_type=F32)
        val = summed * win_ref[:, pl.ds(ch * CW, CW)]
        send3[ch] = val.astype(BF16).reshape(NS, 16, CW)

        def go3(k, c):
            to = sub_at(NS - k if FAR[2] else k)
            pltpu.make_async_remote_copy(
                src_ref=send3.at[ch, to], dst_ref=buf3.at[ch, si],
                send_sem=sends.at[2], recv_sem=r3.at[ch],
                device_id=(fi, to), device_id_type=MESH,
            ).start()
            return c

        lax.fori_loop(1, NS, go3, 0)
        buf3[ch, si] = send3[ch, si]

    def gather(ch):
        wait(buf3.at[ch, pl.ds(0, NS - 1)], r3.at[ch])
        for t in range(8):
            one = buf3[ch, 2 * t].astype(F32)
            two = buf3[ch, 2 * t + 1].astype(F32)
            for c in range(2):
                part = jnp.concatenate([one[8 * c : 8 * c + 8], two[8 * c : 8 * c + 8]], axis=0)
                a_ref[pl.ds(16 * t, 16), pl.ds((2 * ch + c) * CW, CW)] = part.astype(BF16)

    steps = {"r": rows, "f": facets, "g": gather}
    for name, ch in ORDER:
        steps[name](ch)

    def copy4(q):
        return pltpu.make_async_remote_copy(
            src_ref=send4.at[q], dst_ref=buf4.at[m_own],
            send_sem=sends.at[3], recv_sem=r4,
            device_id=(q, dest4), device_id_type=MESH,
        )

    for n in range(NF):
        q = facet_at(NF - 1 - n)
        y = jnp.dot(a_ref[...], w_ref[q], preferred_element_type=F32)

        def part(e):
            return y[8 * e : 8 * e + 8, :NI], y[8 * e : 8 * e + 8, NI:]

        def row(i):
            return jnp.broadcast_to(z_ref[i, pl.ds(q, 1), :], (8, NI))

        zz = (row(2), row(3))
        even, odd = part(14), part(15)
        for e in range(12, -1, -2):
            even = cadd(cmul(even, zz), part(e))
            odd = cadd(cmul(odd, zz), part(e + 1))
        total = cadd(even, cmul(odd, (row(0), row(1))))
        k = ((m_own - so_ref[q]) & 7) + 8 * iota((8, NI), 1)
        keep = jnp.logical_and(k >= ext_ref[0, q], k < SG - ext_ref[1, q])
        both = jnp.concatenate(
            [jnp.where(keep, total[0], 0.0), jnp.where(keep, total[1], 0.0)], axis=0
        )
        send4[q] = both.astype(BF16)
        if n < NF - 1:
            copy4(q).start()
        else:
            @pl.when(is_own4)
            def _():
                buf4[m_own] = send4[q]

            @pl.when(jnp.logical_not(is_own4))
            def _():
                copy4(q).start()

    tw = cs(iota((NF, NI), 0) * iota((NF, NI), 1) * 32)
    wait(buf1.at[:, pl.ds(0, 480), :], sends.at[0])
    wait(buf2.at[:, pl.ds(0, NF - 1)], sends.at[1])
    wait(buf3.at[:, pl.ds(0, NS - 1)], sends.at[2])

    @pl.when(is_own4)
    def _():
        wait(buf4.at[pl.ds(0, NF - 1)], r4)

    @pl.when(jnp.logical_not(is_own4))
    def _():
        wait(buf4, r4)

    got = buf4[...].reshape(128, NI)
    spec = jnp.dot(got, v_ref[0], preferred_element_type=F32) + jnp.dot(
        got, v_ref[1], preferred_element_type=F32
    )
    for m in range(NF):
        re, im = spec[16 * m : 16 * m + 8], spec[16 * m + 8 : 16 * m + 16]
        tp_ref[m, 0] = re[:, :NI] - im[:, NI:]
        tp_ref[m, 1] = re[:, NI:] + im[:, :NI]
    own = so_ref[fi]
    terms = []
    for kap in range(NF):
        got = tp_ref[(own + kap) & 7]
        step = (
            jnp.broadcast_to(tw[0][kap : kap + 1], (8, NI)),
            jnp.broadcast_to(tw[1][kap : kap + 1], (8, NI)),
        )
        terms.append(cmul((got[0], got[1]), step))
    scale = 1.0 / (4096.0 * math.sqrt(SG))
    for n, val in enumerate(dft8(terms)):
        out_ref[0, :, pl.ds(n * NI, NI)] = val[0] * scale
        out_ref[1, :, pl.ds(n * NI, NI)] = val[1] * scale

    @pl.when(is_own4)
    def _():
        wait(buf4.at[pl.ds(0, NF - 1)], sends.at[3])

    @pl.when(jnp.logical_not(is_own4))
    def _():
        wait(buf4, sends.at[3])


def local(slab, window, facet_offsets, subgrid_offsets, row_positions, band_offset, extents):
    hbm = pl.BlockSpec(memory_space=pltpu.MemorySpace.HBM)
    dma = pltpu.SemaphoreType.DMA
    out = pl.pallas_call(
        kernel,
        out_shape=jax.ShapeDtypeStruct((2, 8, SG), F32),
        in_specs=[hbm] * 7,
        out_specs=pl.BlockSpec(memory_space=pltpu.VMEM),
        scratch_shapes=[
            pltpu.VMEM((1, XW), F32),
            pltpu.VMEM((1, ROWS), jnp.int32),
            pltpu.SMEM((NF,), jnp.int32),
            pltpu.SMEM((NF,), jnp.int32),
            pltpu.SMEM((1,), jnp.int32),
            pltpu.SMEM((2, NF), jnp.int32),
            pltpu.VMEM((C, 2 * ROWS, CW), BF16),
            pltpu.VMEM((2, ROWS, 2 * ROWS), BF16),
            pltpu.VMEM((C, NF, 32, CW), BF16),
            pltpu.VMEM((C, NF, 32, CW), BF16),
            pltpu.VMEM((256, 256), BF16),
            pltpu.VMEM((C, NS, 16, CW), BF16),
            pltpu.VMEM((C, NS, 16, CW), BF16),
            pltpu.VMEM((128, 2 * XW), BF16),
            pltpu.VMEM((NF, 2 * XW, 2 * NI), BF16),
            pltpu.VMEM((4, NF, NI), F32),
            pltpu.VMEM((NF, 16, NI), BF16),
            pltpu.VMEM((NF, 16, NI), BF16),
            pltpu.VMEM((2, NI, 2 * NI), BF16),
            pltpu.VMEM((NF, 2, 8, NI), F32),
            dma((4,)), dma((C,)), dma((C,)), dma((C,)), dma, dma((C,)), dma((6,)),
            pltpu.SemaphoreType.REGULAR, pltpu.SemaphoreType.REGULAR,
        ],
        compiler_params=pltpu.CompilerParams(
            collective_id=0, has_side_effects=True, vmem_limit_bytes=63 << 20
        ),
    )(
        slab, window.reshape(1, -1), row_positions.reshape(1, -1),
        facet_offsets, subgrid_offsets, band_offset, extents.T,
    )
    return out.transpose(1, 0, 2)[:, None]


def solution(mesh):
    return jax.shard_map(
        local,
        mesh=mesh,
        in_specs=(P("sub", None, "facet"), P(), P(), P(), P(), P(), P()),
        out_specs=P("sub", "facet", None, None),
        check_vma=False,
    )
```

```python
import math

import jax
import jax.numpy as jnp
from jax import lax
from jax.experimental import pallas as pl
from jax.experimental.pallas import tpu as pltpu
from jax.sharding import PartitionSpec as P

MESH = pl.DeviceIdType.MESH
F32 = jnp.float32
BF16 = jnp.bfloat16
NF = 8
NS = 16
ROWS = 256
XW = 512
NI = 256
SG = 2048
C = 4
CW = XW // C
FAR = (True, True, True)
ORDER = tuple((step, ch) for step in "rfg" for ch in range(C))


def cs(n):
    quad = (n + 8192) >> 14
    th = (n - (quad << 14)).astype(F32) * (2.0 * math.pi / 65536)
    t2 = th * th
    s = th * (1.0 + t2 * (-1.0 / 6 + t2 * (1.0 / 120 - t2 * (1.0 / 5040))))
    c = 1.0 + t2 * (-0.5 + t2 * (1.0 / 24 + t2 * (-1.0 / 720 + t2 * (1.0 / 40320))))
    odd = (quad & 1) == 1
    cos = jnp.where(odd, s, c)
    sin = jnp.where(odd, c, s)
    cos = jnp.where(((quad + 1) & 2) == 2, -cos, cos)
    sin = jnp.where((quad & 2) == 2, -sin, sin)
    return cos, sin


def iota(shape, dim):
    return lax.broadcasted_iota(jnp.int32, shape, dim)


def cmul(a, b):
    return a[0] * b[0] - a[1] * b[1], a[0] * b[1] + a[1] * b[0]


def cadd(a, b):
    return a[0] + b[0], a[1] + b[1]


def csub(a, b):
    return a[0] - b[0], a[1] - b[1]


def times_i(a):
    return -a[1], a[0]


def dft4(x0, x1, x2, x3):
    a, b = cadd(x0, x2), csub(x0, x2)
    c, d = cadd(x1, x3), times_i(csub(x1, x3))
    return cadd(a, c), cadd(b, d), csub(a, c), csub(b, d)


def dft8(t):
    even = dft4(t[0], t[2], t[4], t[6])
    odd = dft4(t[1], t[3], t[5], t[7])
    h = math.sqrt(0.5)
    o1 = ((odd[1][0] - odd[1][1]) * h, (odd[1][0] + odd[1][1]) * h)
    o2 = times_i(odd[2])
    o3 = ((-odd[3][0] - odd[3][1]) * h, (odd[3][0] - odd[3][1]) * h)
    odd = (odd[0], o1, o2, o3)
    return [cadd(e, o) for e, o in zip(even, odd)] + [csub(e, o) for e, o in zip(even, odd)]


def split(v):
    high = v.astype(BF16)
    return high, (v - high.astype(F32)).astype(BF16)


def kernel(
    d_ref, win_hbm, pos_hbm, fo_hbm, so_hbm, band_hbm, ext_hbm, out_ref,
    win_ref, pos_ref, fo_ref, so_ref, band_ref, ext_ref,
    buf1, e_ref, send2, buf2, fb, send3, buf3, a_ref, w_ref, z_ref, send4, buf4, v_ref, tp_ref,
    sends, r1, r2, r3, r4, loc, small, near, far,
):
    fi = lax.axis_index("facet")
    si = lax.axis_index("sub")
    m_own = si >> 1
    jh = si & 1
    dest4 = 2 * fi + jh
    src4 = si >> 1
    is_own4 = fi == src4

    def sub_at(k):
        code = k >> 2
        x = ((si >> 1) + (code ^ (code >> 1))) & 3
        return ((si >> 3) ^ ((k >> 1) & 1)) * 8 + x * 2 + ((si & 1) ^ (k & 1))

    def facet_at(k):
        code = k >> 1
        return (((fi >> 1) + (code ^ (code >> 1))) & 3) * 2 + ((fi & 1) ^ (k & 1))

    beside = (((fi + 2) & 7, si), ((fi + 6) & 7, si), (fi ^ 1, si))
    barrier = pltpu.get_barrier_semaphore()

    def greet(k, c):
        to = sub_at(NS - k)
        pl.semaphore_signal(barrier, inc=1, device_id=(fi, to), device_id_type=MESH)
        return c

    for to in beside:
        pl.semaphore_signal(barrier, inc=1, device_id=to, device_id_type=MESH)
    lax.fori_loop(1, NS, greet, 0)

    smalls = [
        pltpu.make_async_copy(src, dst, small.at[n])
        for n, (src, dst) in enumerate((
            (pos_hbm, pos_ref), (band_hbm, band_ref), (fo_hbm, fo_ref), (so_hbm, so_ref),
            (ext_hbm, ext_ref),
            (win_hbm.at[:, pl.ds(pl.multiple_of(si * XW, XW), XW)], win_ref),
        ))
    ]
    for copy in smalls:
        copy.start()
    slab = d_ref.reshape(32, d_ref.shape[2])

    def own1(ch):
        return pltpu.make_async_copy(
            slab.at[:, pl.ds(pl.multiple_of(si * XW + ch * CW, CW), CW)],
            buf1.at[ch, pl.ds(pl.multiple_of(si * 32, 32), 32), :],
            loc.at[ch],
        )

    for ch in range(C):
        own1(ch).start()

    pl.semaphore_wait(barrier, NS - 1 + 3)

    for ch in range(C):

        def go1(k, c, ch=ch):
            to = sub_at(NS - k if FAR[0] else k)
            pltpu.make_async_remote_copy(
                src_ref=slab.at[:, pl.ds(pl.multiple_of(to * XW + ch * CW, CW), CW)],
                dst_ref=buf1.at[ch, pl.ds(pl.multiple_of(si * 32, 32), 32), :],
                send_sem=sends.at[0], recv_sem=r1.at[ch],
                device_id=(fi, to), device_id_type=MESH,
            ).start()
            return c

        lax.fori_loop(1, NS, go1, 0)

    for to in beside:
        pl.semaphore_signal(near, inc=1, device_id=to, device_id_type=MESH)

    for copy in smalls:
        copy.wait()

    band = band_ref[0]
    pos = pos_ref[...]
    pick = (iota((ROWS, 2 * ROWS), 1) >> 1 == iota((ROWS, 2 * ROWS), 0)).astype(BF16)
    digits = jnp.concatenate([pos >> 8, pos & 255], axis=0).astype(F32).astype(BF16)
    digits = jnp.dot(digits, pick, preferred_element_type=F32).astype(jnp.int32)
    twice = digits[0:1] * 256 + digits[1:2]
    turn = (iota((1, 2 * ROWS), 1) & 1) * 16384

    def row_table(g, c):
        cos, sin = cs(twice * (iota((8, 2 * ROWS), 0) + (8 * g + band)) - turn)
        high, low = split(jnp.concatenate([cos, -sin], axis=0))
        at = pl.ds(pl.multiple_of(16 * g, 16), 16)
        e_ref[0, at, :] = high
        e_ref[1, at, :] = low
        return c

    lax.fori_loop(0, 16, row_table, 0)

    lane = iota((1, 256), 1)
    off = jnp.zeros((1, 256), jnp.int32)
    for b in range(NF):
        off = jnp.where((lane >> 5) == b, fo_ref[b], off)

    def facet_table(g, c):
        row = iota((32, 256), 0)
        col = iota((32, 256), 1)
        cos, sin = cs(jnp.broadcast_to(off * (g * 8192), (32, 256)))
        rc, cc = (row >> 3) & 1, (col >> 3) & 1
        val = jnp.where(rc == cc, cos, jnp.where(rc == 0, sin, -sin))
        val = jnp.where(((row ^ col) & 0b10111) == 0, val, 0.0)
        fb[pl.ds(pl.multiple_of(32 * g, 32), 32), :] = val.astype(BF16)
        return c

    lax.fori_loop(0, NF, facet_table, 0)

    pl.semaphore_wait(near, 3)
    pl.semaphore_signal(far, inc=1, device_id=beside[1], device_id_type=MESH)

    def first_freq(q):
        o = so_ref[q]
        return o + ((m_own - o) & 7)

    lane = iota((1, 128), 1)
    freq = jnp.zeros((1, 128), jnp.int32)
    for q in range(NF):
        freq = jnp.where(lane == q, first_freq(q), freq)

    def column_table(ac, c):
        step = 32
        a0 = ac * step
        base = cs((iota((step, NI), 0) + a0) * iota((step, NI), 1) * 8)
        ph = cs((iota((step, 128), 0) + a0) * freq)
        row = (ac // (CW // step)) * (2 * CW) + (ac % (CW // step)) * step
        top = pl.ds(pl.multiple_of(row, step), step)
        low = pl.ds(pl.multiple_of(row + CW, step), step)
        for q in range(NF):
            pq = (
                jnp.broadcast_to(ph[0][:, q : q + 1], (step, NI)),
                jnp.broadcast_to(ph[1][:, q : q + 1], (step, NI)),
            )
            cos, sin = cmul(base, pq)
            cos = cos.astype(BF16)
            sin = sin.astype(BF16)
            w_ref[q, top, pl.ds(0, NI)] = cos
            w_ref[q, top, pl.ds(NI, NI)] = -sin
            w_ref[q, low, pl.ds(0, NI)] = sin
            w_ref[q, low, pl.ds(NI, NI)] = cos
        return c

    lax.fori_loop(0, XW // 32, column_table, 0)

    fq = jnp.zeros((NF, NI), jnp.int32)
    for q in range(NF):
        fq = jnp.where(iota((NF, NI), 0) == q, first_freq(q), fq)
    fq = fq + 8 * iota((NF, NI), 1)
    z1 = cs(fq * 512)
    z2 = cs(fq * 1024)
    z_ref[0], z_ref[1] = z1[0], -z1[1]
    z_ref[2], z_ref[3] = z2[0], -z2[1]

    def sub_table(g, c):
        cos, sin = cs((iota((32, NI), 0) + 32 * g) * iota((32, NI), 1) * 256)
        at = pl.ds(pl.multiple_of(32 * g, 32), 32)
        for n, part in enumerate((cos, sin)):
            high, low = split(part)
            v_ref[0, at, pl.ds(n * NI, NI)] = high
            v_ref[1, at, pl.ds(n * NI, NI)] = low
        return c

    lax.fori_loop(0, 8, sub_table, 0)
    pl.semaphore_wait(far, 1)

    def wait(ref, sem):
        pltpu.make_async_copy(ref, ref, sem).wait()

    def rows(ch):
        own1(ch).wait()
        wait(buf1.at[ch, pl.ds(0, 480), :], r1.at[ch])
        data = buf1[ch]
        val = jnp.dot(e_ref[0], data, preferred_element_type=F32) + jnp.dot(
            e_ref[1], data, preferred_element_type=F32
        )
        send2[ch] = val.astype(BF16).reshape(NF, 32, CW)

        def go2(k, c):
            to = facet_at(NF - k if FAR[1] else k)
            pltpu.make_async_remote_copy(
                src_ref=send2.at[ch, to], dst_ref=buf2.at[ch, fi],
                send_sem=sends.at[1], recv_sem=r2.at[ch],
                device_id=(to, si), device_id_type=MESH,
            ).start()
            return c

        lax.fori_loop(1, NF, go2, 0)
        buf2[ch, fi] = send2[ch, fi]

    def facets(ch):
        wait(buf2.at[ch, pl.ds(0, NF - 1)], r2.at[ch])
        summed = jnp.dot(fb[...], buf2[ch].reshape(256, CW), preferred_element_type=F32)
        val = summed * win_ref[:, pl.ds(ch * CW, CW)]
        send3[ch] = val.astype(BF16).reshape(NS, 16, CW)

        def go3(k, c):
            to = sub_at(NS - k if FAR[2] else k)
            pltpu.make_async_remote_copy(
                src_ref=send3.at[ch, to], dst_ref=buf3.at[ch, si],
                send_sem=sends.at[2], recv_sem=r3.at[ch],
                device_id=(fi, to), device_id_type=MESH,
            ).start()
            return c

        lax.fori_loop(1, NS, go3, 0)
        buf3[ch, si] = send3[ch, si]

    def gather(ch):
        wait(buf3.at[ch, pl.ds(0, NS - 1)], r3.at[ch])
        for t in range(8):
            one = buf3[ch, 2 * t].astype(F32)
            two = buf3[ch, 2 * t + 1].astype(F32)
            for c in range(2):
                part = jnp.concatenate([one[8 * c : 8 * c + 8], two[8 * c : 8 * c + 8]], axis=0)
                a_ref[pl.ds(16 * t, 16), pl.ds((2 * ch + c) * CW, CW)] = part.astype(BF16)

    steps = {"r": rows, "f": facets, "g": gather}
    for name, ch in ORDER:
        steps[name](ch)

    def copy4(q):
        return pltpu.make_async_remote_copy(
            src_ref=send4.at[q], dst_ref=buf4.at[m_own],
            send_sem=sends.at[3], recv_sem=r4,
            device_id=(q, dest4), device_id_type=MESH,
        )

    for n in range(NF):
        q = facet_at(NF - 1 - n)
        y = jnp.dot(a_ref[...], w_ref[q], preferred_element_type=F32)

        def part(e):
            return y[8 * e : 8 * e + 8, :NI], y[8 * e : 8 * e + 8, NI:]

        def row(i):
            return jnp.broadcast_to(z_ref[i, pl.ds(q, 1), :], (8, NI))

        zz = (row(2), row(3))
        even, odd = part(14), part(15)
        for e in range(12, -1, -2):
            even = cadd(cmul(even, zz), part(e))
            odd = cadd(cmul(odd, zz), part(e + 1))
        total = cadd(even, cmul(odd, (row(0), row(1))))
        k = ((m_own - so_ref[q]) & 7) + 8 * iota((8, NI), 1)
        keep = jnp.logical_and(k >= ext_ref[0, q], k < SG - ext_ref[1, q])
        both = jnp.concatenate(
            [jnp.where(keep, total[0], 0.0), jnp.where(keep, total[1], 0.0)], axis=0
        )
        send4[q] = both.astype(BF16)
        if n < NF - 1:
            copy4(q).start()
        else:
            @pl.when(is_own4)
            def _():
                buf4[m_own] = send4[q]

            @pl.when(jnp.logical_not(is_own4))
            def _():
                copy4(q).start()

    tw = cs(iota((NF, NI), 0) * iota((NF, NI), 1) * 32)
    wait(buf1.at[:, pl.ds(0, 480), :], sends.at[0])
    wait(buf2.at[:, pl.ds(0, NF - 1)], sends.at[1])
    wait(buf3.at[:, pl.ds(0, NS - 1)], sends.at[2])

    @pl.when(is_own4)
    def _():
        wait(buf4.at[pl.ds(0, NF - 1)], r4)

    @pl.when(jnp.logical_not(is_own4))
    def _():
        wait(buf4, r4)

    got = buf4[...].reshape(128, NI)
    spec = jnp.dot(got, v_ref[0], preferred_element_type=F32) + jnp.dot(
        got, v_ref[1], preferred_element_type=F32
    )
    for m in range(NF):
        re, im = spec[16 * m : 16 * m + 8], spec[16 * m + 8 : 16 * m + 16]
        tp_ref[m, 0] = re[:, :NI] - im[:, NI:]
        tp_ref[m, 1] = re[:, NI:] + im[:, :NI]
    own = so_ref[fi]
    terms = []
    for kap in range(NF):
        got = tp_ref[(own + kap) & 7]
        step = (
            jnp.broadcast_to(tw[0][kap : kap + 1], (8, NI)),
            jnp.broadcast_to(tw[1][kap : kap + 1], (8, NI)),
        )
        terms.append(cmul((got[0], got[1]), step))
    scale = 1.0 / (4096.0 * math.sqrt(SG))
    for n, val in enumerate(dft8(terms)):
        out_ref[0, :, pl.ds(n * NI, NI)] = val[0] * scale
        out_ref[1, :, pl.ds(n * NI, NI)] = val[1] * scale

    @pl.when(is_own4)
    def _():
        wait(buf4.at[pl.ds(0, NF - 1)], sends.at[3])

    @pl.when(jnp.logical_not(is_own4))
    def _():
        wait(buf4, sends.at[3])


def local(slab, window, facet_offsets, subgrid_offsets, row_positions, band_offset, extents):
    hbm = pl.BlockSpec(memory_space=pltpu.MemorySpace.HBM)
    dma = pltpu.SemaphoreType.DMA
    out = pl.pallas_call(
        kernel,
        out_shape=jax.ShapeDtypeStruct((2, 8, SG), F32),
        in_specs=[hbm] * 7,
        out_specs=pl.BlockSpec(memory_space=pltpu.VMEM),
        scratch_shapes=[
            pltpu.VMEM((1, XW), F32),
            pltpu.VMEM((1, ROWS), jnp.int32),
            pltpu.SMEM((NF,), jnp.int32),
            pltpu.SMEM((NF,), jnp.int32),
            pltpu.SMEM((1,), jnp.int32),
            pltpu.SMEM((2, NF), jnp.int32),
            pltpu.VMEM((C, 2 * ROWS, CW), BF16),
            pltpu.VMEM((2, ROWS, 2 * ROWS), BF16),
            pltpu.VMEM((C, NF, 32, CW), BF16),
            pltpu.VMEM((C, NF, 32, CW), BF16),
            pltpu.VMEM((256, 256), BF16),
            pltpu.VMEM((C, NS, 16, CW), BF16),
            pltpu.VMEM((C, NS, 16, CW), BF16),
            pltpu.VMEM((128, 2 * XW), BF16),
            pltpu.VMEM((NF, 2 * XW, 2 * NI), BF16),
            pltpu.VMEM((4, NF, NI), F32),
            pltpu.VMEM((NF, 16, NI), BF16),
            pltpu.VMEM((NF, 16, NI), BF16),
            pltpu.VMEM((2, NI, 2 * NI), BF16),
            pltpu.VMEM((NF, 2, 8, NI), F32),
            dma((4,)), dma((C,)), dma((C,)), dma((C,)), dma, dma((C,)), dma((6,)),
            pltpu.SemaphoreType.REGULAR, pltpu.SemaphoreType.REGULAR,
        ],
        compiler_params=pltpu.CompilerParams(
            collective_id=0, has_side_effects=True, vmem_limit_bytes=40 << 20
        ),
    )(*(
        x if x.size == 1 else pltpu.with_memory_space_constraint(x, pltpu.MemorySpace.HBM)
        for x in (
            slab, window.reshape(1, -1), row_positions.reshape(1, -1),
            facet_offsets, subgrid_offsets, band_offset, extents.T,
        )
    ))
    return out.transpose(1, 0, 2)[:, None]


def solution(mesh):
    return jax.shard_map(
        local,
        mesh=mesh,
        in_specs=(P("sub", None, "facet"), P(), P(), P(), P(), P(), P()),
        out_specs=P("sub", "facet", None, None),
        check_vma=False,
    )
```

```python
import math

import jax
import jax.numpy as jnp
from jax import lax
from jax.experimental import pallas as pl
from jax.experimental.pallas import tpu as pltpu
from jax.sharding import PartitionSpec as P

MESH = pl.DeviceIdType.MESH
F32 = jnp.float32
BF16 = jnp.bfloat16
NF = 8
NS = 16
ROWS = 256
XW = 512
NI = 256
SG = 2048
CUT = 2
C = 4
CW = XW // C
ORDER = tuple((step, ch) for step in "rfg" for ch in range(C))


def cs(n):
    quad = (n + 8192) >> 14
    th = (n - (quad << 14)).astype(F32) * (2.0 * math.pi / 65536)
    t2 = th * th
    s = th * (1.0 + t2 * (-1.0 / 6 + t2 * (1.0 / 120 - t2 * (1.0 / 5040))))
    c = 1.0 + t2 * (-0.5 + t2 * (1.0 / 24 + t2 * (-1.0 / 720 + t2 * (1.0 / 40320))))
    odd = (quad & 1) == 1
    cos = jnp.where(odd, s, c)
    sin = jnp.where(odd, c, s)
    cos = jnp.where(((quad + 1) & 2) == 2, -cos, cos)
    sin = jnp.where((quad & 2) == 2, -sin, sin)
    return cos, sin


def iota(shape, dim):
    return lax.broadcasted_iota(jnp.int32, shape, dim)


def cmul(a, b):
    return a[0] * b[0] - a[1] * b[1], a[0] * b[1] + a[1] * b[0]


def cadd(a, b):
    return a[0] + b[0], a[1] + b[1]


def csub(a, b):
    return a[0] - b[0], a[1] - b[1]


def times_i(a):
    return -a[1], a[0]


def dft4(x0, x1, x2, x3):
    a, b = cadd(x0, x2), csub(x0, x2)
    c, d = cadd(x1, x3), times_i(csub(x1, x3))
    return cadd(a, c), cadd(b, d), csub(a, c), csub(b, d)


def dft8(t):
    even = dft4(t[0], t[2], t[4], t[6])
    odd = dft4(t[1], t[3], t[5], t[7])
    h = math.sqrt(0.5)
    o1 = ((odd[1][0] - odd[1][1]) * h, (odd[1][0] + odd[1][1]) * h)
    o2 = times_i(odd[2])
    o3 = ((-odd[3][0] - odd[3][1]) * h, (odd[3][0] - odd[3][1]) * h)
    odd = (odd[0], o1, o2, o3)
    return [cadd(e, o) for e, o in zip(even, odd)] + [csub(e, o) for e, o in zip(even, odd)]


def split(v):
    high = v.astype(BF16)
    return high, (v - high.astype(F32)).astype(BF16)


def kernel(
    d_ref, win_hbm, pos_hbm, fo_hbm, so_hbm, band_hbm, ext_hbm, out_ref,
    win_lo, win_hi, pos_ref, fo_ref, so_ref, band_ref, ext_ref,
    buf1, e_ref, send2, buf2, fb, send3, buf3, a_ref, w_ref, z_ref, send4, buf4, v_ref, tp_ref,
    sends, r1, r2, r3, r4, loc, small, near, far, y_ref,
):
    fi = lax.axis_index("facet")
    si = lax.axis_index("sub")
    m_own = si & 7
    jh = si >> 3
    dest4 = 2 * fi + jh
    is_own4 = dest4 == si

    def sub_at(k):
        code = k >> 2
        x = ((si >> 1) + (code ^ (code >> 1))) & 3
        return ((si >> 3) ^ ((k >> 1) & 1)) * 8 + x * 2 + ((si & 1) ^ (k & 1))

    def facet_at(k):
        code = k >> 1
        return (((fi >> 1) + (code ^ (code >> 1))) & 3) * 2 + ((fi & 1) ^ (k & 1))

    beside = (((fi + 2) & 7, si), ((fi + 6) & 7, si), (fi ^ 1, si))
    barrier = pltpu.get_barrier_semaphore()

    def greet(k, c):
        to = sub_at(NS - k)
        pl.semaphore_signal(barrier, inc=1, device_id=(fi, to), device_id_type=MESH)
        return c

    for f, s in beside:
        for to in ((f, s ^ 8), (f, s)):
            pl.semaphore_signal(barrier, inc=1, device_id=to, device_id_type=MESH)
    lax.fori_loop(1, NS, greet, 0)

    smalls = [
        pltpu.make_async_copy(src, dst, small.at[n])
        for n, (src, dst) in enumerate((
            (pos_hbm, pos_ref), (band_hbm, band_ref), (fo_hbm, fo_ref), (so_hbm, so_ref),
            (ext_hbm, ext_ref),
            (win_hbm.at[:, pl.ds(pl.multiple_of(m_own * XW, XW), XW)], win_lo),
            (win_hbm.at[:, pl.ds(pl.multiple_of((m_own + 8) * XW, XW), XW)], win_hi),
        ))
    ]
    for copy in smalls:
        copy.start()
    slab = d_ref.reshape(32, d_ref.shape[2])

    def own1(ch):
        return pltpu.make_async_copy(
            slab.at[:, pl.ds(pl.multiple_of(si * XW + ch * CW, CW), CW)],
            buf1.at[ch, pl.ds(pl.multiple_of(si * 32, 32), 32), :],
            loc.at[ch],
        )

    for ch in range(C):
        own1(ch).start()

    pl.semaphore_wait(barrier, NS - 1 + 6)

    for ch in range(C):

        def go1(k, c, ch=ch):
            to = sub_at(NS - k)
            pltpu.make_async_remote_copy(
                src_ref=slab.at[:, pl.ds(pl.multiple_of(to * XW + ch * CW, CW), CW)],
                dst_ref=buf1.at[ch, pl.ds(pl.multiple_of(si * 32, 32), 32), :],
                send_sem=sends.at[0], recv_sem=r1.at[ch],
                device_id=(fi, to), device_id_type=MESH,
            ).start()
            return c

        lax.fori_loop(1, NS, go1, 0)

    for to in beside:
        pl.semaphore_signal(near, inc=1, device_id=to, device_id_type=MESH)

    for copy in smalls:
        copy.wait()

    band = band_ref[0]
    pos = pos_ref[...]
    pick = (iota((ROWS, 2 * ROWS), 1) >> 1 == iota((ROWS, 2 * ROWS), 0)).astype(BF16)
    digits = jnp.concatenate([pos >> 8, pos & 255], axis=0).astype(F32).astype(BF16)
    digits = jnp.dot(digits, pick, preferred_element_type=F32).astype(jnp.int32)
    twice = digits[0:1] * 256 + digits[1:2]
    turn = (iota((1, 2 * ROWS), 1) & 1) * 16384

    def row_table(g, c):
        cos, sin = cs(twice * (iota((8, 2 * ROWS), 0) + (8 * g + band)) - turn)
        high, low = split(jnp.concatenate([cos, -sin], axis=0))
        at = pl.ds(pl.multiple_of(16 * g, 16), 16)
        e_ref[0, at, :] = high
        e_ref[1, at, :] = low
        return c

    lax.fori_loop(0, 16, row_table, 0)

    lane = iota((1, 128), 1)
    off = jnp.zeros((1, 128), jnp.int32)
    for b in range(NF):
        off = jnp.where((lane >> 4) == b, fo_ref[b], off)

    def facet_table(g, c):
        row = iota((16, 128), 0)
        col = iota((16, 128), 1)
        cos, sin = cs(jnp.broadcast_to(off * (g * 8192), (16, 128)))
        rc, cc = (row >> 3) & 1, (col >> 3) & 1
        val = jnp.where(rc == cc, cos, jnp.where(rc == 0, sin, -sin))
        val = jnp.where(((row ^ col) & 0b111) == 0, val, 0.0)
        fb[pl.ds(pl.multiple_of(16 * g, 16), 16), :] = val.astype(BF16)
        return c

    lax.fori_loop(0, NF, facet_table, 0)

    pl.semaphore_wait(near, 3)
    pl.semaphore_signal(far, inc=1, device_id=beside[1], device_id_type=MESH)

    def first_freq(q):
        o = so_ref[q]
        return o + ((m_own - o) & 7)

    lane = iota((1, 128), 1)
    freq = jnp.zeros((1, 128), jnp.int32)
    for q in range(NF):
        freq = jnp.where(lane == q, first_freq(q), freq)

    def column_table(ac, c):
        step = 32
        a0 = ac * step
        base = cs((iota((step, NI), 0) + a0) * iota((step, NI), 1) * 8)
        ph = cs((iota((step, 128), 0) + a0) * freq)
        row = (ac // (CW // step)) * (2 * CW) + (ac % (CW // step)) * step
        top = pl.ds(pl.multiple_of(row, step), step)
        low = pl.ds(pl.multiple_of(row + CW, step), step)
        for q in range(NF):
            pq = (
                jnp.broadcast_to(ph[0][:, q : q + 1], (step, NI)),
                jnp.broadcast_to(ph[1][:, q : q + 1], (step, NI)),
            )
            cos, sin = cmul(base, pq)
            cos = cos.astype(BF16)
            sin = sin.astype(BF16)
            w_ref[q, top, pl.ds(0, NI)] = cos
            w_ref[q, top, pl.ds(NI, NI)] = -sin
            w_ref[q, low, pl.ds(0, NI)] = sin
            w_ref[q, low, pl.ds(NI, NI)] = cos
        return c

    lax.fori_loop(0, XW // 32, column_table, 0)

    fq = jnp.zeros((NF, NI), jnp.int32)
    for q in range(NF):
        fq = jnp.where(iota((NF, NI), 0) == q, first_freq(q), fq)
    fq = fq + 8 * iota((NF, NI), 1)
    z1 = cs(fq * 512)
    z2 = cs(fq * 1024)
    z_ref[0], z_ref[1] = z1[0], -z1[1]
    z_ref[2], z_ref[3] = z2[0], -z2[1]

    def sub_table(g, c):
        cos, sin = cs((iota((32, NI), 0) + 32 * g) * iota((32, NI), 1) * 256)
        at = pl.ds(pl.multiple_of(32 * g, 32), 32)
        for n, part in enumerate((cos, sin)):
            high, low = split(part)
            v_ref[0, at, pl.ds(n * NI, NI)] = high
            v_ref[1, at, pl.ds(n * NI, NI)] = low
        return c

    lax.fori_loop(0, 8, sub_table, 0)
    pl.semaphore_wait(far, 1)

    def wait(ref, sem):
        pltpu.make_async_copy(ref, ref, sem).wait()

    def rows(ch):
        own1(ch).wait()
        wait(buf1.at[ch, pl.ds(0, 480), :], r1.at[ch])
        data = buf1[ch]
        val = jnp.dot(e_ref[0], data, preferred_element_type=F32) + jnp.dot(
            e_ref[1], data, preferred_element_type=F32
        )
        send2[ch] = val.astype(BF16).reshape(NS, 16, CW)

        def go2(n, c):
            k = NS - n
            f = facet_at(k >> 1)
            half = jh ^ (k & 1)
            pltpu.make_async_remote_copy(
                src_ref=send2.at[ch, 2 * f + half], dst_ref=buf2.at[ch, 8 * jh + fi],
                send_sem=sends.at[1], recv_sem=r2.at[ch],
                device_id=(f, 8 * half + m_own), device_id_type=MESH,
            ).start()
            return c

        lax.fori_loop(1, NS, go2, 0)
        buf2[ch, 8 * jh + fi] = send2[ch, dest4]

    def facets(ch):
        wait(buf2.at[ch, pl.ds(0, NS - 1)], r2.at[ch])
        for half, win in enumerate((win_lo, win_hi)):
            data = buf2[ch, pl.ds(8 * half, 8)].reshape(128, CW)
            val = jnp.dot(fb[...], data, preferred_element_type=F32) * win[:, pl.ds(ch * CW, CW)]
            send3[ch, :, half] = val.astype(BF16).reshape(NF, 16, CW)

        def go3(n, c):
            k = NF - n
            code = k >> 1
            x = ((m_own >> 1) + (code ^ (code >> 1))) & 3
            to = 2 * x + ((m_own & 1) ^ (k & 1))
            pltpu.make_async_remote_copy(
                src_ref=send3.at[ch, to], dst_ref=buf3.at[ch, m_own],
                send_sem=sends.at[2], recv_sem=r3.at[ch],
                device_id=(fi, 8 * jh + to), device_id_type=MESH,
            ).start()
            return c

        lax.fori_loop(1, NF, go3, 0)
        buf3[ch, m_own] = send3[ch, m_own]

    def gather(ch):
        wait(buf3.at[ch, pl.ds(0, NF - 1)], r3.at[ch])
        for t in range(8):
            one = buf3[ch, (2 * t) % 8, t // 4].astype(F32)
            two = buf3[ch, (2 * t + 1) % 8, t // 4].astype(F32)
            for c in range(2):
                part = jnp.concatenate([one[8 * c : 8 * c + 8], two[8 * c : 8 * c + 8]], axis=0)
                a_ref[pl.ds(16 * t, 16), pl.ds((2 * ch + c) * CW, CW)] = part.astype(BF16)

    steps = {"r": rows, "f": facets, "g": gather}
    for name, ch in ORDER:
        steps[name](ch)
        if (name, ch) == ("g", CUT - 1):
            for n in range(NF):
                y_ref[n] = jnp.dot(
                    a_ref[:, : 2 * CUT * CW], w_ref[facet_at(NF - 1 - n), : 2 * CUT * CW, :],
                    preferred_element_type=F32,
                )

    def copy4(q):
        return pltpu.make_async_remote_copy(
            src_ref=send4.at[q], dst_ref=buf4.at[m_own],
            send_sem=sends.at[3], recv_sem=r4,
            device_id=(q, dest4), device_id_type=MESH,
        )

    for n in range(NF):
        q = facet_at(NF - 1 - n)
        y = y_ref[n] + jnp.dot(
            a_ref[:, 2 * CUT * CW :], w_ref[q, 2 * CUT * CW :, :], preferred_element_type=F32
        )

        def part(e):
            return y[8 * e : 8 * e + 8, :NI], y[8 * e : 8 * e + 8, NI:]

        def row(i):
            return jnp.broadcast_to(z_ref[i, pl.ds(q, 1), :], (8, NI))

        zz = (row(2), row(3))
        even, odd = part(14), part(15)
        for e in range(12, -1, -2):
            even = cadd(cmul(even, zz), part(e))
            odd = cadd(cmul(odd, zz), part(e + 1))
        total = cadd(even, cmul(odd, (row(0), row(1))))
        k = ((m_own - so_ref[q]) & 7) + 8 * iota((8, NI), 1)
        keep = jnp.logical_and(k >= ext_ref[0, q], k < SG - ext_ref[1, q])
        both = jnp.concatenate(
            [jnp.where(keep, total[0], 0.0), jnp.where(keep, total[1], 0.0)], axis=0
        )
        send4[q] = both.astype(BF16)
        if n < NF - 1:
            copy4(q).start()
        else:
            @pl.when(is_own4)
            def _():
                buf4[m_own] = send4[q]

            @pl.when(jnp.logical_not(is_own4))
            def _():
                copy4(q).start()

    tw = cs(iota((NF, NI), 0) * iota((NF, NI), 1) * 32)
    wait(buf1.at[:, pl.ds(0, 480), :], sends.at[0])
    wait(buf2.at[:, pl.ds(0, NS - 1)], sends.at[1])
    wait(buf3.at[:, pl.ds(0, NF - 1)], sends.at[2])

    @pl.when(is_own4)
    def _():
        wait(buf4.at[pl.ds(0, NF - 1)], r4)

    @pl.when(jnp.logical_not(is_own4))
    def _():
        wait(buf4, r4)

    got = buf4[...].reshape(128, NI)
    spec = jnp.dot(got, v_ref[0], preferred_element_type=F32) + jnp.dot(
        got, v_ref[1], preferred_element_type=F32
    )
    for m in range(NF):
        re, im = spec[16 * m : 16 * m + 8], spec[16 * m + 8 : 16 * m + 16]
        tp_ref[m, 0] = re[:, :NI] - im[:, NI:]
        tp_ref[m, 1] = re[:, NI:] + im[:, :NI]
    own = so_ref[fi]
    terms = []
    for kap in range(NF):
        got = tp_ref[(own + kap) & 7]
        step = (
            jnp.broadcast_to(tw[0][kap : kap + 1], (8, NI)),
            jnp.broadcast_to(tw[1][kap : kap + 1], (8, NI)),
        )
        terms.append(cmul((got[0], got[1]), step))
    scale = 1.0 / (4096.0 * math.sqrt(SG))
    for n, val in enumerate(dft8(terms)):
        out_ref[0, :, pl.ds(n * NI, NI)] = val[0] * scale
        out_ref[1, :, pl.ds(n * NI, NI)] = val[1] * scale

    @pl.when(is_own4)
    def _():
        wait(buf4.at[pl.ds(0, NF - 1)], sends.at[3])

    @pl.when(jnp.logical_not(is_own4))
    def _():
        wait(buf4, sends.at[3])


def local(slab, window, facet_offsets, subgrid_offsets, row_positions, band_offset, extents):
    hbm = pl.BlockSpec(memory_space=pltpu.MemorySpace.HBM)
    dma = pltpu.SemaphoreType.DMA
    out = pl.pallas_call(
        kernel,
        out_shape=jax.ShapeDtypeStruct((2, 8, SG), F32),
        in_specs=[hbm] * 7,
        out_specs=pl.BlockSpec(memory_space=pltpu.VMEM),
        scratch_shapes=[
            pltpu.VMEM((1, XW), F32),
            pltpu.VMEM((1, XW), F32),
            pltpu.VMEM((1, ROWS), jnp.int32),
            pltpu.SMEM((NF,), jnp.int32),
            pltpu.SMEM((NF,), jnp.int32),
            pltpu.SMEM((1,), jnp.int32),
            pltpu.SMEM((2, NF), jnp.int32),
            pltpu.VMEM((C, 2 * ROWS, CW), BF16),
            pltpu.VMEM((2, ROWS, 2 * ROWS), BF16),
            pltpu.VMEM((C, NS, 16, CW), BF16),
            pltpu.VMEM((C, NS, 16, CW), BF16),
            pltpu.VMEM((128, 128), BF16),
            pltpu.VMEM((C, NF, 2, 16, CW), BF16),
            pltpu.VMEM((C, NF, 2, 16, CW), BF16),
            pltpu.VMEM((128, 2 * XW), BF16),
            pltpu.VMEM((NF, 2 * XW, 2 * NI), BF16),
            pltpu.VMEM((4, NF, NI), F32),
            pltpu.VMEM((NF, 16, NI), BF16),
            pltpu.VMEM((NF, 16, NI), BF16),
            pltpu.VMEM((2, NI, 2 * NI), BF16),
            pltpu.VMEM((NF, 2, 8, NI), F32),
            dma((4,)), dma((C,)), dma((C,)), dma((C,)), dma, dma((C,)), dma((7,)),
            pltpu.SemaphoreType.REGULAR, pltpu.SemaphoreType.REGULAR,
            pltpu.VMEM((NF, 128, 2 * NI), F32),
        ],
        compiler_params=pltpu.CompilerParams(
            collective_id=0, has_side_effects=True, vmem_limit_bytes=40 << 20
        ),
    )(*(
        x if x.size == 1 else pltpu.with_memory_space_constraint(x, pltpu.MemorySpace.HBM)
        for x in (
            slab, window.reshape(1, -1), row_positions.reshape(1, -1),
            facet_offsets, subgrid_offsets, band_offset, extents.T,
        )
    ))
    return out.transpose(1, 0, 2)[:, None]


def solution(mesh):
    return jax.shard_map(
        local,
        mesh=mesh,
        in_specs=(P("sub", None, "facet"), P(), P(), P(), P(), P(), P()),
        out_specs=P("sub", "facet", None, None),
        check_vma=False,
    )
```

```python
import math

import jax
import jax.numpy as jnp
from jax import lax
from jax.experimental import pallas as pl
from jax.experimental.pallas import tpu as pltpu
from jax.sharding import PartitionSpec as P

MESH = pl.DeviceIdType.MESH
F32 = jnp.float32
BF16 = jnp.bfloat16
NF = 8
NS = 16
ROWS = 256
XW = 512
NI = 256
SG = 2048
CUT = 2
C = 4
CW = XW // C
ORDER = tuple((step, ch) for step in "rfg" for ch in range(C))


def cs(n):
    quad = (n + 8192) >> 14
    th = (n - (quad << 14)).astype(F32) * (2.0 * math.pi / 65536)
    t2 = th * th
    s = th * (1.0 + t2 * (-1.0 / 6 + t2 * (1.0 / 120 - t2 * (1.0 / 5040))))
    c = 1.0 + t2 * (-0.5 + t2 * (1.0 / 24 + t2 * (-1.0 / 720 + t2 * (1.0 / 40320))))
    odd = (quad & 1) == 1
    cos = jnp.where(odd, s, c)
    sin = jnp.where(odd, c, s)
    cos = jnp.where(((quad + 1) & 2) == 2, -cos, cos)
    sin = jnp.where((quad & 2) == 2, -sin, sin)
    return cos, sin


def iota(shape, dim):
    return lax.broadcasted_iota(jnp.int32, shape, dim)


def cmul(a, b):
    return a[0] * b[0] - a[1] * b[1], a[0] * b[1] + a[1] * b[0]


def cadd(a, b):
    return a[0] + b[0], a[1] + b[1]


def csub(a, b):
    return a[0] - b[0], a[1] - b[1]


def times_i(a):
    return -a[1], a[0]


def dft4(x0, x1, x2, x3):
    a, b = cadd(x0, x2), csub(x0, x2)
    c, d = cadd(x1, x3), times_i(csub(x1, x3))
    return cadd(a, c), cadd(b, d), csub(a, c), csub(b, d)


def dft8(t):
    even = dft4(t[0], t[2], t[4], t[6])
    odd = dft4(t[1], t[3], t[5], t[7])
    h = math.sqrt(0.5)
    o1 = ((odd[1][0] - odd[1][1]) * h, (odd[1][0] + odd[1][1]) * h)
    o2 = times_i(odd[2])
    o3 = ((-odd[3][0] - odd[3][1]) * h, (odd[3][0] - odd[3][1]) * h)
    odd = (odd[0], o1, o2, o3)
    return [cadd(e, o) for e, o in zip(even, odd)] + [csub(e, o) for e, o in zip(even, odd)]


def split(v):
    high = v.astype(BF16)
    return high, (v - high.astype(F32)).astype(BF16)


def kernel(
    d_ref, win_hbm, pos_hbm, fo_hbm, so_hbm, band_hbm, ext_hbm, out_ref,
    win_lo, win_hi, pos_ref, fo_ref, so_ref, band_ref, ext_ref,
    buf1, e_ref, send2, buf2, fb, send3, buf3, a_ref, w_ref, z_ref, send4, buf4, v_ref, tp_ref,
    sends, r1, r2, r3, r4, loc, small, near, far, y_ref, slab,
):
    fi = lax.axis_index("facet")
    si = lax.axis_index("sub")
    m_own = si & 7
    jh = si >> 3
    dest4 = 2 * fi + jh
    is_own4 = dest4 == si

    def sub_at(k):
        code = k >> 2
        x = ((si >> 1) + (code ^ (code >> 1))) & 3
        return ((si >> 3) ^ ((k >> 1) & 1)) * 8 + x * 2 + ((si & 1) ^ (k & 1))

    def facet_at(k):
        code = k >> 1
        return (((fi >> 1) + (code ^ (code >> 1))) & 3) * 2 + ((fi & 1) ^ (k & 1))

    beside = (((fi + 2) & 7, si), ((fi + 6) & 7, si), (fi ^ 1, si))
    barrier = pltpu.get_barrier_semaphore()

    def greet(k, c):
        to = sub_at(NS - k)
        pl.semaphore_signal(barrier, inc=1, device_id=(fi, to), device_id_type=MESH)
        return c

    for f, s in beside:
        for to in ((f, s ^ 8), (f, s)):
            pl.semaphore_signal(barrier, inc=1, device_id=to, device_id_type=MESH)
    lax.fori_loop(1, NS, greet, 0)

    smalls = [
        pltpu.make_async_copy(src, dst, small.at[n])
        for n, (src, dst) in enumerate((
            (pos_hbm, pos_ref), (band_hbm, band_ref), (fo_hbm, fo_ref), (so_hbm, so_ref),
            (ext_hbm, ext_ref),
            (win_hbm.at[:, pl.ds(pl.multiple_of(m_own * XW, XW), XW)], win_lo),
            (win_hbm.at[:, pl.ds(pl.multiple_of((m_own + 8) * XW, XW), XW)], win_hi),
        ))
    ]
    for copy in smalls:
        copy.start()
    staged = pltpu.make_async_copy(d_ref.reshape(32, d_ref.shape[2]), slab, small.at[7])
    staged.start()

    def own1(ch):
        return pltpu.make_async_copy(
            slab.at[:, pl.ds(pl.multiple_of(si * XW + ch * CW, CW), CW)],
            buf1.at[ch, pl.ds(pl.multiple_of(si * 32, 32), 32), :],
            loc.at[ch],
        )


    pl.semaphore_wait(barrier, NS - 1 + 6)

    staged.wait()
    for ch in range(C):
        own1(ch).start()

    for ch in range(C):

        def go1(k, c, ch=ch):
            to = sub_at(NS - k)
            pltpu.make_async_remote_copy(
                src_ref=slab.at[:, pl.ds(pl.multiple_of(to * XW + ch * CW, CW), CW)],
                dst_ref=buf1.at[ch, pl.ds(pl.multiple_of(si * 32, 32), 32), :],
                send_sem=sends.at[0], recv_sem=r1.at[ch],
                device_id=(fi, to), device_id_type=MESH,
            ).start()
            return c

        lax.fori_loop(1, NS, go1, 0)

    for to in beside:
        pl.semaphore_signal(near, inc=1, device_id=to, device_id_type=MESH)

    for copy in smalls:
        copy.wait()

    band = band_ref[0]
    pos = pos_ref[...]
    pick = (iota((ROWS, 2 * ROWS), 1) >> 1 == iota((ROWS, 2 * ROWS), 0)).astype(BF16)
    digits = jnp.concatenate([pos >> 8, pos & 255], axis=0).astype(F32).astype(BF16)
    digits = jnp.dot(digits, pick, preferred_element_type=F32).astype(jnp.int32)
    twice = digits[0:1] * 256 + digits[1:2]
    turn = (iota((1, 2 * ROWS), 1) & 1) * 16384

    def row_table(g, c):
        cos, sin = cs(twice * (iota((8, 2 * ROWS), 0) + (8 * g + band)) - turn)
        high, low = split(jnp.concatenate([cos, -sin], axis=0))
        at = pl.ds(pl.multiple_of(16 * g, 16), 16)
        e_ref[0, at, :] = high
        e_ref[1, at, :] = low
        return c

    lax.fori_loop(0, 16, row_table, 0)

    lane = iota((1, 128), 1)
    off = jnp.zeros((1, 128), jnp.int32)
    for b in range(NF):
        off = jnp.where((lane >> 4) == b, fo_ref[b], off)

    def facet_table(g, c):
        row = iota((16, 128), 0)
        col = iota((16, 128), 1)
        cos, sin = cs(jnp.broadcast_to(off * (g * 8192), (16, 128)))
        rc, cc = (row >> 3) & 1, (col >> 3) & 1
        val = jnp.where(rc == cc, cos, jnp.where(rc == 0, sin, -sin))
        val = jnp.where(((row ^ col) & 0b111) == 0, val, 0.0)
        fb[pl.ds(pl.multiple_of(16 * g, 16), 16), :] = val.astype(BF16)
        return c

    lax.fori_loop(0, NF, facet_table, 0)

    pl.semaphore_wait(near, 3)
    pl.semaphore_signal(far, inc=1, device_id=beside[1], device_id_type=MESH)

    def first_freq(q):
        o = so_ref[q]
        return o + ((m_own - o) & 7)

    lane = iota((1, 128), 1)
    freq = jnp.zeros((1, 128), jnp.int32)
    for q in range(NF):
        freq = jnp.where(lane == q, first_freq(q), freq)

    def column_table(ac, c):
        step = 32
        a0 = ac * step
        base = cs((iota((step, NI), 0) + a0) * iota((step, NI), 1) * 8)
        ph = cs((iota((step, 128), 0) + a0) * freq)
        row = (ac // (CW // step)) * (2 * CW) + (ac % (CW // step)) * step
        top = pl.ds(pl.multiple_of(row, step), step)
        low = pl.ds(pl.multiple_of(row + CW, step), step)
        for q in range(NF):
            pq = (
                jnp.broadcast_to(ph[0][:, q : q + 1], (step, NI)),
                jnp.broadcast_to(ph[1][:, q : q + 1], (step, NI)),
            )
            cos, sin = cmul(base, pq)
            cos = cos.astype(BF16)
            sin = sin.astype(BF16)
            w_ref[q, top, pl.ds(0, NI)] = cos
            w_ref[q, top, pl.ds(NI, NI)] = -sin
            w_ref[q, low, pl.ds(0, NI)] = sin
            w_ref[q, low, pl.ds(NI, NI)] = cos
        return c

    lax.fori_loop(0, XW // 32, column_table, 0)

    fq = jnp.zeros((NF, NI), jnp.int32)
    for q in range(NF):
        fq = jnp.where(iota((NF, NI), 0) == q, first_freq(q), fq)
    fq = fq + 8 * iota((NF, NI), 1)
    z1 = cs(fq * 512)
    z2 = cs(fq * 1024)
    z_ref[0], z_ref[1] = z1[0], -z1[1]
    z_ref[2], z_ref[3] = z2[0], -z2[1]

    def sub_table(g, c):
        cos, sin = cs((iota((32, NI), 0) + 32 * g) * iota((32, NI), 1) * 256)
        at = pl.ds(pl.multiple_of(32 * g, 32), 32)
        for n, part in enumerate((cos, sin)):
            high, low = split(part)
            v_ref[0, at, pl.ds(n * NI, NI)] = high
            v_ref[1, at, pl.ds(n * NI, NI)] = low
        return c

    lax.fori_loop(0, 8, sub_table, 0)
    pl.semaphore_wait(far, 1)

    def wait(ref, sem):
        pltpu.make_async_copy(ref, ref, sem).wait()

    def rows(ch):
        own1(ch).wait()
        wait(buf1.at[ch, pl.ds(0, 480), :], r1.at[ch])
        data = buf1[ch]
        val = jnp.dot(e_ref[0], data, preferred_element_type=F32) + jnp.dot(
            e_ref[1], data, preferred_element_type=F32
        )
        send2[ch] = val.astype(BF16).reshape(NS, 16, CW)

        def go2(n, c):
            k = NS - n
            f = facet_at(k >> 1)
            half = jh ^ (k & 1)
            pltpu.make_async_remote_copy(
                src_ref=send2.at[ch, 2 * f + half], dst_ref=buf2.at[ch, 8 * jh + fi],
                send_sem=sends.at[1], recv_sem=r2.at[ch],
                device_id=(f, 8 * half + m_own), device_id_type=MESH,
            ).start()
            return c

        lax.fori_loop(1, NS, go2, 0)
        buf2[ch, 8 * jh + fi] = send2[ch, dest4]

    def facets(ch):
        wait(buf2.at[ch, pl.ds(0, NS - 1)], r2.at[ch])
        for half, win in enumerate((win_lo, win_hi)):
            data = buf2[ch, pl.ds(8 * half, 8)].reshape(128, CW)
            val = jnp.dot(fb[...], data, preferred_element_type=F32) * win[:, pl.ds(ch * CW, CW)]
            send3[ch, :, half] = val.astype(BF16).reshape(NF, 16, CW)

        def go3(n, c):
            k = NF - n
            code = k >> 1
            x = ((m_own >> 1) + (code ^ (code >> 1))) & 3
            to = 2 * x + ((m_own & 1) ^ (k & 1))
            pltpu.make_async_remote_copy(
                src_ref=send3.at[ch, to], dst_ref=buf3.at[ch, m_own],
                send_sem=sends.at[2], recv_sem=r3.at[ch],
                device_id=(fi, 8 * jh + to), device_id_type=MESH,
            ).start()
            return c

        lax.fori_loop(1, NF, go3, 0)
        buf3[ch, m_own] = send3[ch, m_own]

    def gather(ch):
        wait(buf3.at[ch, pl.ds(0, NF - 1)], r3.at[ch])
        for t in range(8):
            one = buf3[ch, (2 * t) % 8, t // 4].astype(F32)
            two = buf3[ch, (2 * t + 1) % 8, t // 4].astype(F32)
            for c in range(2):
                part = jnp.concatenate([one[8 * c : 8 * c + 8], two[8 * c : 8 * c + 8]], axis=0)
                a_ref[pl.ds(16 * t, 16), pl.ds((2 * ch + c) * CW, CW)] = part.astype(BF16)

    steps = {"r": rows, "f": facets, "g": gather}
    for name, ch in ORDER:
        steps[name](ch)
        if (name, ch) == ("g", CUT - 1):
            for n in range(NF):
                y_ref[n] = jnp.dot(
                    a_ref[:, : 2 * CUT * CW], w_ref[facet_at(NF - 1 - n), : 2 * CUT * CW, :],
                    preferred_element_type=F32,
                )

    def copy4(q):
        return pltpu.make_async_remote_copy(
            src_ref=send4.at[q], dst_ref=buf4.at[m_own],
            send_sem=sends.at[3], recv_sem=r4,
            device_id=(q, dest4), device_id_type=MESH,
        )

    for n in range(NF):
        q = facet_at(NF - 1 - n)
        y = y_ref[n] + jnp.dot(
            a_ref[:, 2 * CUT * CW :], w_ref[q, 2 * CUT * CW :, :], preferred_element_type=F32
        )

        def part(e):
            return y[8 * e : 8 * e + 8, :NI], y[8 * e : 8 * e + 8, NI:]

        def row(i):
            return jnp.broadcast_to(z_ref[i, pl.ds(q, 1), :], (8, NI))

        zz = (row(2), row(3))
        even, odd = part(14), part(15)
        for e in range(12, -1, -2):
            even = cadd(cmul(even, zz), part(e))
            odd = cadd(cmul(odd, zz), part(e + 1))
        total = cadd(even, cmul(odd, (row(0), row(1))))
        k = ((m_own - so_ref[q]) & 7) + 8 * iota((8, NI), 1)
        keep = jnp.logical_and(k >= ext_ref[0, q], k < SG - ext_ref[1, q])
        both = jnp.concatenate(
            [jnp.where(keep, total[0], 0.0), jnp.where(keep, total[1], 0.0)], axis=0
        )
        send4[q] = both.astype(BF16)
        if n < NF - 1:
            copy4(q).start()
        else:
            @pl.when(is_own4)
            def _():
                buf4[m_own] = send4[q]

            @pl.when(jnp.logical_not(is_own4))
            def _():
                copy4(q).start()

    tw = cs(iota((NF, NI), 0) * iota((NF, NI), 1) * 32)
    wait(buf1.at[:, pl.ds(0, 480), :], sends.at[0])
    wait(buf2.at[:, pl.ds(0, NS - 1)], sends.at[1])
    wait(buf3.at[:, pl.ds(0, NF - 1)], sends.at[2])

    @pl.when(is_own4)
    def _():
        wait(buf4.at[pl.ds(0, NF - 1)], r4)

    @pl.when(jnp.logical_not(is_own4))
    def _():
        wait(buf4, r4)

    got = buf4[...].reshape(128, NI)
    spec = jnp.dot(got, v_ref[0], preferred_element_type=F32) + jnp.dot(
        got, v_ref[1], preferred_element_type=F32
    )
    for m in range(NF):
        re, im = spec[16 * m : 16 * m + 8], spec[16 * m + 8 : 16 * m + 16]
        tp_ref[m, 0] = re[:, :NI] - im[:, NI:]
        tp_ref[m, 1] = re[:, NI:] + im[:, :NI]
    own = so_ref[fi]
    terms = []
    for kap in range(NF):
        got = tp_ref[(own + kap) & 7]
        step = (
            jnp.broadcast_to(tw[0][kap : kap + 1], (8, NI)),
            jnp.broadcast_to(tw[1][kap : kap + 1], (8, NI)),
        )
        terms.append(cmul((got[0], got[1]), step))
    scale = 1.0 / (4096.0 * math.sqrt(SG))
    for n, val in enumerate(dft8(terms)):
        out_ref[0, :, pl.ds(n * NI, NI)] = val[0] * scale
        out_ref[1, :, pl.ds(n * NI, NI)] = val[1] * scale

    @pl.when(is_own4)
    def _():
        wait(buf4.at[pl.ds(0, NF - 1)], sends.at[3])

    @pl.when(jnp.logical_not(is_own4))
    def _():
        wait(buf4, sends.at[3])


def local(slab, window, facet_offsets, subgrid_offsets, row_positions, band_offset, extents):
    hbm = pl.BlockSpec(memory_space=pltpu.MemorySpace.HBM)
    dma = pltpu.SemaphoreType.DMA
    out = pl.pallas_call(
        kernel,
        out_shape=jax.ShapeDtypeStruct((2, 8, SG), F32),
        in_specs=[hbm] * 7,
        out_specs=pl.BlockSpec(memory_space=pltpu.VMEM),
        scratch_shapes=[
            pltpu.VMEM((1, XW), F32),
            pltpu.VMEM((1, XW), F32),
            pltpu.VMEM((1, ROWS), jnp.int32),
            pltpu.SMEM((NF,), jnp.int32),
            pltpu.SMEM((NF,), jnp.int32),
            pltpu.SMEM((1,), jnp.int32),
            pltpu.SMEM((2, NF), jnp.int32),
            pltpu.VMEM((C, 2 * ROWS, CW), BF16),
            pltpu.VMEM((2, ROWS, 2 * ROWS), BF16),
            pltpu.VMEM((C, NS, 16, CW), BF16),
            pltpu.VMEM((C, NS, 16, CW), BF16),
            pltpu.VMEM((128, 128), BF16),
            pltpu.VMEM((C, NF, 2, 16, CW), BF16),
            pltpu.VMEM((C, NF, 2, 16, CW), BF16),
            pltpu.VMEM((128, 2 * XW), BF16),
            pltpu.VMEM((NF, 2 * XW, 2 * NI), BF16),
            pltpu.VMEM((4, NF, NI), F32),
            pltpu.VMEM((NF, 16, NI), BF16),
            pltpu.VMEM((NF, 16, NI), BF16),
            pltpu.VMEM((2, NI, 2 * NI), BF16),
            pltpu.VMEM((NF, 2, 8, NI), F32),
            dma((4,)), dma((C,)), dma((C,)), dma((C,)), dma, dma((C,)), dma((8,)),
            pltpu.SemaphoreType.REGULAR, pltpu.SemaphoreType.REGULAR,
            pltpu.VMEM((NF, 128, 2 * NI), F32),
            pltpu.VMEM((32, slab.shape[2]), BF16),
        ],
        compiler_params=pltpu.CompilerParams(
            collective_id=0, has_side_effects=True, vmem_limit_bytes=40 << 20
        ),
    )(*(
        x if x.size == 1 else pltpu.with_memory_space_constraint(x, pltpu.MemorySpace.HBM)
        for x in (
            slab, window.reshape(1, -1), row_positions.reshape(1, -1),
            facet_offsets, subgrid_offsets, band_offset, extents.T,
        )
    ))
    return out.transpose(1, 0, 2)[:, None]


def solution(mesh):
    return jax.shard_map(
        local,
        mesh=mesh,
        in_specs=(P("sub", None, "facet"), P(), P(), P(), P(), P(), P()),
        out_specs=P("sub", "facet", None, None),
        check_vma=False,
    )
```

```python
import math

import jax
import jax.numpy as jnp
from jax import lax
from jax.experimental import pallas as pl
from jax.experimental.pallas import tpu as pltpu
from jax.sharding import PartitionSpec as P

MESH = pl.DeviceIdType.MESH
F32 = jnp.float32
BF16 = jnp.bfloat16
NF = 8
NS = 16
ROWS = 256
XW = 512
NI = 256
SG = 2048
CUT = 2
C = 4
CW = XW // C
ORDER = tuple((step, ch) for step in "rfg" for ch in range(C))


def cs(n):
    quad = (n + 8192) >> 14
    th = (n - (quad << 14)).astype(F32) * (2.0 * math.pi / 65536)
    t2 = th * th
    s = th * (1.0 + t2 * (-1.0 / 6 + t2 * (1.0 / 120 - t2 * (1.0 / 5040))))
    c = 1.0 + t2 * (-0.5 + t2 * (1.0 / 24 + t2 * (-1.0 / 720 + t2 * (1.0 / 40320))))
    odd = (quad & 1) == 1
    cos = jnp.where(odd, s, c)
    sin = jnp.where(odd, c, s)
    cos = jnp.where(((quad + 1) & 2) == 2, -cos, cos)
    sin = jnp.where((quad & 2) == 2, -sin, sin)
    return cos, sin


def iota(shape, dim):
    return lax.broadcasted_iota(jnp.int32, shape, dim)


def cmul(a, b):
    return a[0] * b[0] - a[1] * b[1], a[0] * b[1] + a[1] * b[0]


def cadd(a, b):
    return a[0] + b[0], a[1] + b[1]


def csub(a, b):
    return a[0] - b[0], a[1] - b[1]


def times_i(a):
    return -a[1], a[0]


def dft4(x0, x1, x2, x3):
    a, b = cadd(x0, x2), csub(x0, x2)
    c, d = cadd(x1, x3), times_i(csub(x1, x3))
    return cadd(a, c), cadd(b, d), csub(a, c), csub(b, d)


def dft8(t):
    even = dft4(t[0], t[2], t[4], t[6])
    odd = dft4(t[1], t[3], t[5], t[7])
    h = math.sqrt(0.5)
    o1 = ((odd[1][0] - odd[1][1]) * h, (odd[1][0] + odd[1][1]) * h)
    o2 = times_i(odd[2])
    o3 = ((-odd[3][0] - odd[3][1]) * h, (odd[3][0] - odd[3][1]) * h)
    odd = (odd[0], o1, o2, o3)
    return [cadd(e, o) for e, o in zip(even, odd)] + [csub(e, o) for e, o in zip(even, odd)]


def split(v):
    high = v.astype(BF16)
    return high, (v - high.astype(F32)).astype(BF16)


def kernel(
    d_ref, win_hbm, pos_hbm, fo_hbm, so_hbm, band_hbm, ext_hbm, out_ref,
    win_lo, win_hi, pos_ref, fo_ref, so_ref, band_ref, ext_ref,
    buf1, e_ref, send2, buf2, fb, send3, buf3, a_ref, w_ref, z_ref, send4, buf4, v_ref, tp_ref,
    sends, r1, r2, r3, r4, loc, small, near, far, y_ref, slab,
):
    fi = lax.axis_index("facet")
    si = lax.axis_index("sub")
    m_own = si & 7
    jh = si >> 3
    dest4 = 2 * fi + jh
    is_own4 = dest4 == si

    staged = pltpu.make_async_copy(d_ref.reshape(32, d_ref.shape[2]), slab, small.at[7])
    staged.start()

    def sub_at(k):
        code = k >> 2
        x = ((si >> 1) + (code ^ (code >> 1))) & 3
        return ((si >> 3) ^ ((k >> 1) & 1)) * 8 + x * 2 + ((si & 1) ^ (k & 1))

    def facet_at(k):
        code = k >> 1
        return (((fi >> 1) + (code ^ (code >> 1))) & 3) * 2 + ((fi & 1) ^ (k & 1))

    beside = (((fi + 2) & 7, si), ((fi + 6) & 7, si), (fi ^ 1, si))
    barrier = pltpu.get_barrier_semaphore()

    def greet(k, c):
        to = sub_at(NS - k)
        pl.semaphore_signal(barrier, inc=1, device_id=(fi, to), device_id_type=MESH)
        return c

    for f, s in beside:
        for to in ((f, s ^ 8), (f, s)):
            pl.semaphore_signal(barrier, inc=1, device_id=to, device_id_type=MESH)
    lax.fori_loop(1, NS, greet, 0)

    smalls = [
        pltpu.make_async_copy(src, dst, small.at[n])
        for n, (src, dst) in enumerate((
            (pos_hbm, pos_ref), (band_hbm, band_ref), (fo_hbm, fo_ref), (so_hbm, so_ref),
            (ext_hbm, ext_ref),
            (win_hbm.at[:, pl.ds(pl.multiple_of(m_own * XW, XW), XW)], win_lo),
            (win_hbm.at[:, pl.ds(pl.multiple_of((m_own + 8) * XW, XW), XW)], win_hi),
        ))
    ]
    for copy in smalls:
        copy.start()

    def own1(ch):
        return pltpu.make_async_copy(
            slab.at[:, pl.ds(pl.multiple_of(si * XW + ch * CW, CW), CW)],
            buf1.at[ch, pl.ds(pl.multiple_of(si * 32, 32), 32), :],
            loc.at[ch],
        )


    pl.semaphore_wait(barrier, NS - 1 + 6)

    staged.wait()
    for ch in range(C):
        own1(ch).start()

    for ch in range(C):

        def go1(k, c, ch=ch):
            to = sub_at(NS - k)
            pltpu.make_async_remote_copy(
                src_ref=slab.at[:, pl.ds(pl.multiple_of(to * XW + ch * CW, CW), CW)],
                dst_ref=buf1.at[ch, pl.ds(pl.multiple_of(si * 32, 32), 32), :],
                send_sem=sends.at[0], recv_sem=r1.at[ch],
                device_id=(fi, to), device_id_type=MESH,
            ).start()
            return c

        lax.fori_loop(1, NS, go1, 0)

    for to in beside:
        pl.semaphore_signal(near, inc=1, device_id=to, device_id_type=MESH)

    for copy in smalls:
        copy.wait()

    band = band_ref[0]
    pos = pos_ref[...]
    pick = (iota((ROWS, 2 * ROWS), 1) >> 1 == iota((ROWS, 2 * ROWS), 0)).astype(BF16)
    digits = jnp.concatenate([pos >> 8, pos & 255], axis=0).astype(F32).astype(BF16)
    digits = jnp.dot(digits, pick, preferred_element_type=F32).astype(jnp.int32)
    twice = digits[0:1] * 256 + digits[1:2]
    turn = (iota((1, 2 * ROWS), 1) & 1) * 16384

    def row_table(g, c):
        cos, sin = cs(twice * (iota((8, 2 * ROWS), 0) + (8 * g + band)) - turn)
        high, low = split(jnp.concatenate([cos, -sin], axis=0))
        at = pl.ds(pl.multiple_of(16 * g, 16), 16)
        e_ref[0, at, :] = high
        e_ref[1, at, :] = low
        return c

    lax.fori_loop(0, 16, row_table, 0)

    lane = iota((1, 128), 1)
    off = jnp.zeros((1, 128), jnp.int32)
    for b in range(NF):
        off = jnp.where((lane >> 4) == b, fo_ref[b], off)

    def facet_table(g, c):
        row = iota((16, 128), 0)
        col = iota((16, 128), 1)
        cos, sin = cs(jnp.broadcast_to(off * (g * 8192), (16, 128)))
        rc, cc = (row >> 3) & 1, (col >> 3) & 1
        val = jnp.where(rc == cc, cos, jnp.where(rc == 0, sin, -sin))
        val = jnp.where(((row ^ col) & 0b111) == 0, val, 0.0)
        fb[pl.ds(pl.multiple_of(16 * g, 16), 16), :] = val.astype(BF16)
        return c

    lax.fori_loop(0, NF, facet_table, 0)

    pl.semaphore_wait(near, 3)
    pl.semaphore_signal(far, inc=1, device_id=beside[1], device_id_type=MESH)

    def first_freq(q):
        o = so_ref[q]
        return o + ((m_own - o) & 7)

    lane = iota((1, 128), 1)
    freq = jnp.zeros((1, 128), jnp.int32)
    for q in range(NF):
        freq = jnp.where(lane == q, first_freq(q), freq)

    def column_table(ac, c):
        step = 32
        a0 = ac * step
        base = cs((iota((step, NI), 0) + a0) * iota((step, NI), 1) * 8)
        ph = cs((iota((step, 128), 0) + a0) * freq)
        row = (ac // (CW // step)) * (2 * CW) + (ac % (CW // step)) * step
        top = pl.ds(pl.multiple_of(row, step), step)
        low = pl.ds(pl.multiple_of(row + CW, step), step)
        for q in range(NF):
            pq = (
                jnp.broadcast_to(ph[0][:, q : q + 1], (step, NI)),
                jnp.broadcast_to(ph[1][:, q : q + 1], (step, NI)),
            )
            cos, sin = cmul(base, pq)
            cos = cos.astype(BF16)
            sin = sin.astype(BF16)
            w_ref[q, top, pl.ds(0, NI)] = cos
            w_ref[q, top, pl.ds(NI, NI)] = -sin
            w_ref[q, low, pl.ds(0, NI)] = sin
            w_ref[q, low, pl.ds(NI, NI)] = cos
        return c

    lax.fori_loop(0, XW // 32, column_table, 0)

    fq = jnp.zeros((NF, NI), jnp.int32)
    for q in range(NF):
        fq = jnp.where(iota((NF, NI), 0) == q, first_freq(q), fq)
    fq = fq + 8 * iota((NF, NI), 1)
    z1 = cs(fq * 512)
    z2 = cs(fq * 1024)
    z_ref[0], z_ref[1] = z1[0], -z1[1]
    z_ref[2], z_ref[3] = z2[0], -z2[1]

    def sub_table(g, c):
        cos, sin = cs((iota((32, NI), 0) + 32 * g) * iota((32, NI), 1) * 256)
        at = pl.ds(pl.multiple_of(32 * g, 32), 32)
        for n, part in enumerate((cos, sin)):
            high, low = split(part)
            v_ref[0, at, pl.ds(n * NI, NI)] = high
            v_ref[1, at, pl.ds(n * NI, NI)] = low
        return c

    lax.fori_loop(0, 8, sub_table, 0)
    pl.semaphore_wait(far, 1)

    def wait(ref, sem):
        pltpu.make_async_copy(ref, ref, sem).wait()

    def rows(ch):
        own1(ch).wait()
        wait(buf1.at[ch, pl.ds(0, 480), :], r1.at[ch])
        data = buf1[ch]
        val = jnp.dot(e_ref[0], data, preferred_element_type=F32) + jnp.dot(
            e_ref[1], data, preferred_element_type=F32
        )
        send2[ch] = val.astype(BF16).reshape(NS, 16, CW)

        def go2(n, c):
            k = NS - n
            f = facet_at(k >> 1)
            half = jh ^ (k & 1)
            pltpu.make_async_remote_copy(
                src_ref=send2.at[ch, 2 * f + half], dst_ref=buf2.at[ch, 8 * jh + fi],
                send_sem=sends.at[1], recv_sem=r2.at[ch],
                device_id=(f, 8 * half + m_own), device_id_type=MESH,
            ).start()
            return c

        lax.fori_loop(1, NS, go2, 0)
        buf2[ch, 8 * jh + fi] = send2[ch, dest4]

    def facets(ch):
        wait(buf2.at[ch, pl.ds(0, NS - 1)], r2.at[ch])
        for half, win in enumerate((win_lo, win_hi)):
            data = buf2[ch, pl.ds(8 * half, 8)].reshape(128, CW)
            val = jnp.dot(fb[...], data, preferred_element_type=F32) * win[:, pl.ds(ch * CW, CW)]
            send3[ch, :, half] = val.astype(BF16).reshape(NF, 16, CW)

        def go3(n, c):
            k = NF - n
            code = k >> 1
            x = ((m_own >> 1) + (code ^ (code >> 1))) & 3
            to = 2 * x + ((m_own & 1) ^ (k & 1))
            pltpu.make_async_remote_copy(
                src_ref=send3.at[ch, to], dst_ref=buf3.at[ch, m_own],
                send_sem=sends.at[2], recv_sem=r3.at[ch],
                device_id=(fi, 8 * jh + to), device_id_type=MESH,
            ).start()
            return c

        lax.fori_loop(1, NF, go3, 0)
        buf3[ch, m_own] = send3[ch, m_own]

    def gather(ch):
        wait(buf3.at[ch, pl.ds(0, NF - 1)], r3.at[ch])
        for t in range(8):
            one = buf3[ch, (2 * t) % 8, t // 4].astype(F32)
            two = buf3[ch, (2 * t + 1) % 8, t // 4].astype(F32)
            for c in range(2):
                part = jnp.concatenate([one[8 * c : 8 * c + 8], two[8 * c : 8 * c + 8]], axis=0)
                a_ref[pl.ds(16 * t, 16), pl.ds((2 * ch + c) * CW, CW)] = part.astype(BF16)

    steps = {"r": rows, "f": facets, "g": gather}
    for name, ch in ORDER:
        steps[name](ch)
        if (name, ch) == ("g", CUT - 1):
            for n in range(NF):
                y_ref[n] = jnp.dot(
                    a_ref[:, : 2 * CUT * CW], w_ref[facet_at(NF - 1 - n), : 2 * CUT * CW, :],
                    preferred_element_type=F32,
                )

    def copy4(q):
        return pltpu.make_async_remote_copy(
            src_ref=send4.at[q], dst_ref=buf4.at[m_own],
            send_sem=sends.at[3], recv_sem=r4,
            device_id=(q, dest4), device_id_type=MESH,
        )

    for n in range(NF):
        q = facet_at(NF - 1 - n)
        y = y_ref[n] + jnp.dot(
            a_ref[:, 2 * CUT * CW :], w_ref[q, 2 * CUT * CW :, :], preferred_element_type=F32
        )

        def part(e):
            return y[8 * e : 8 * e + 8, :NI], y[8 * e : 8 * e + 8, NI:]

        def row(i):
            return jnp.broadcast_to(z_ref[i, pl.ds(q, 1), :], (8, NI))

        zz = (row(2), row(3))
        even, odd = part(14), part(15)
        for e in range(12, -1, -2):
            even = cadd(cmul(even, zz), part(e))
            odd = cadd(cmul(odd, zz), part(e + 1))
        total = cadd(even, cmul(odd, (row(0), row(1))))
        k = ((m_own - so_ref[q]) & 7) + 8 * iota((8, NI), 1)
        keep = jnp.logical_and(k >= ext_ref[0, q], k < SG - ext_ref[1, q])
        both = jnp.concatenate(
            [jnp.where(keep, total[0], 0.0), jnp.where(keep, total[1], 0.0)], axis=0
        )
        send4[q] = both.astype(BF16)
        if n < NF - 1:
            copy4(q).start()
        else:
            @pl.when(is_own4)
            def _():
                buf4[m_own] = send4[q]

            @pl.when(jnp.logical_not(is_own4))
            def _():
                copy4(q).start()

    tw = cs(iota((NF, NI), 0) * iota((NF, NI), 1) * 32)
    wait(buf1.at[:, pl.ds(0, 480), :], sends.at[0])
    wait(buf2.at[:, pl.ds(0, NS - 1)], sends.at[1])
    wait(buf3.at[:, pl.ds(0, NF - 1)], sends.at[2])

    @pl.when(is_own4)
    def _():
        wait(buf4.at[pl.ds(0, NF - 1)], r4)

    @pl.when(jnp.logical_not(is_own4))
    def _():
        wait(buf4, r4)

    got = buf4[...].reshape(128, NI)
    spec = jnp.dot(got, v_ref[0], preferred_element_type=F32) + jnp.dot(
        got, v_ref[1], preferred_element_type=F32
    )
    for m in range(NF):
        re, im = spec[16 * m : 16 * m + 8], spec[16 * m + 8 : 16 * m + 16]
        tp_ref[m, 0] = re[:, :NI] - im[:, NI:]
        tp_ref[m, 1] = re[:, NI:] + im[:, :NI]
    own = so_ref[fi]
    terms = []
    for kap in range(NF):
        got = tp_ref[(own + kap) & 7]
        step = (
            jnp.broadcast_to(tw[0][kap : kap + 1], (8, NI)),
            jnp.broadcast_to(tw[1][kap : kap + 1], (8, NI)),
        )
        terms.append(cmul((got[0], got[1]), step))
    scale = 1.0 / (4096.0 * math.sqrt(SG))
    for n, val in enumerate(dft8(terms)):
        out_ref[0, :, pl.ds(n * NI, NI)] = val[0] * scale
        out_ref[1, :, pl.ds(n * NI, NI)] = val[1] * scale

    @pl.when(is_own4)
    def _():
        wait(buf4.at[pl.ds(0, NF - 1)], sends.at[3])

    @pl.when(jnp.logical_not(is_own4))
    def _():
        wait(buf4, sends.at[3])


def local(slab, window, facet_offsets, subgrid_offsets, row_positions, band_offset, extents):
    hbm = pl.BlockSpec(memory_space=pltpu.MemorySpace.HBM)
    dma = pltpu.SemaphoreType.DMA
    out = pl.pallas_call(
        kernel,
        out_shape=jax.ShapeDtypeStruct((2, 8, SG), F32),
        in_specs=[hbm] * 7,
        out_specs=pl.BlockSpec(memory_space=pltpu.VMEM),
        scratch_shapes=[
            pltpu.VMEM((1, XW), F32),
            pltpu.VMEM((1, XW), F32),
            pltpu.VMEM((1, ROWS), jnp.int32),
            pltpu.SMEM((NF,), jnp.int32),
            pltpu.SMEM((NF,), jnp.int32),
            pltpu.SMEM((1,), jnp.int32),
            pltpu.SMEM((2, NF), jnp.int32),
            pltpu.VMEM((C, 2 * ROWS, CW), BF16),
            pltpu.VMEM((2, ROWS, 2 * ROWS), BF16),
            pltpu.VMEM((C, NS, 16, CW), BF16),
            pltpu.VMEM((C, NS, 16, CW), BF16),
            pltpu.VMEM((128, 128), BF16),
            pltpu.VMEM((C, NF, 2, 16, CW), BF16),
            pltpu.VMEM((C, NF, 2, 16, CW), BF16),
            pltpu.VMEM((128, 2 * XW), BF16),
            pltpu.VMEM((NF, 2 * XW, 2 * NI), BF16),
            pltpu.VMEM((4, NF, NI), F32),
            pltpu.VMEM((NF, 16, NI), BF16),
            pltpu.VMEM((NF, 16, NI), BF16),
            pltpu.VMEM((2, NI, 2 * NI), BF16),
            pltpu.VMEM((NF, 2, 8, NI), F32),
            dma((4,)), dma((C,)), dma((C,)), dma((C,)), dma, dma((C,)), dma((8,)),
            pltpu.SemaphoreType.REGULAR, pltpu.SemaphoreType.REGULAR,
            pltpu.VMEM((NF, 128, 2 * NI), F32),
            pltpu.VMEM((32, slab.shape[2]), BF16),
        ],
        compiler_params=pltpu.CompilerParams(
            collective_id=0, has_side_effects=True, vmem_limit_bytes=40 << 20
        ),
    )(*(
        x if x.size == 1 else pltpu.with_memory_space_constraint(x, pltpu.MemorySpace.HBM)
        for x in (
            slab, window.reshape(1, -1), row_positions.reshape(1, -1),
            facet_offsets, subgrid_offsets, band_offset, extents.T,
        )
    ))
    return out.transpose(1, 0, 2)[:, None]


def solution(mesh):
    return jax.shard_map(
        local,
        mesh=mesh,
        in_specs=(P("sub", None, "facet"), P(), P(), P(), P(), P(), P()),
        out_specs=P("sub", "facet", None, None),
        check_vma=False,
    )
```
